512 devices in a mesh: row: 8 (over y), chan: 16 (over z, core), dp: 4 (over x).
Axes of the slice: x: 4, y: 8, z: 8, core: 2. Of those that a mesh axis runs over, the one named last changes fastest.
Arguments:
- features_in: bfloat16 [4, 144, 64, 2048], P('dp', 'row', None, 'chan'), may hold values from -6 to 6
- depth_weights: bfloat16 [3, 3, 3, 2048], P(None, None, None, 'chan'), may hold values from -2 to 2
- point_weights: bfloat16 [4, 2048, 256], P(None, 'chan'), may hold values from -0.125 to 0.125
- proj_weights: bfloat16 [4, 256, 256], replicated, may hold values from -0.1875 to 0.1875
- cotangent: bfloat16 [4, 144, 64, 256], P('dp', 'row', 'chan'), may hold values from -18 to 18
Outputs:
- output: bfloat16 [4, 144, 64, 256], P('dp', 'row', 'chan')
- grad_input: bfloat16 [4, 144, 64, 2048], P('dp', 'row', None, 'chan')
- grad_depth: float32 [3, 3, 3, 2048], P(None, None, None, 'chan')
- grad_point: float32 [4, 2048, 256], P(None, 'chan')
- grad_proj: float32 [4, 256, 256], replicated
The draws below stay inside these ranges and needn't reach their ends.
All inputs are finite; a program needn't handle non-finite values.
Results may differ from the reference program's by a relative error of at most 0.0059.
Values may be sent and summed in bfloat16 or wider, within the bound.
A program may use at most 64 MiB of HBM per device.

```python
import math
import jax
import jax.numpy as jnp
from jax import lax

C = 2048
F = 256
BASE_DILATION = 12
COLS = 64
H = 144
SAMPLES = 4


def block_levels(key, shape, pieces, low, largest):
    def one(dim, shards_of):
        draws = jax.random.uniform(jax.random.fold_in(jax.random.fold_in(key, 6), dim), (shards_of,), jnp.float32, low / len(pieces), largest / len(pieces))
        return jnp.repeat(jnp.exp(draws), shape[dim] // shards_of).reshape((-1,) + (1,) * (len(shape) - dim - 1))

    factor_of = one(*pieces[0])
    for cut in pieces[1:]:
        factor_of = factor_of * one(*cut)
    return factor_of


def bell_draw(stream_key, shape, deviation, reach, shards=(), kind=jnp.bfloat16):
    loudness = block_levels(stream_key, shape, shards, -0.22, 0.18) if shards else 1.0
    result = jax.random.normal(stream_key, shape, jnp.float32) * deviation * loudness
    return jnp.minimum(jnp.maximum(result, -reach), reach).astype(kind)


def setup_inputs(seed: int = 0) -> dict:
    key_of = jax.random.split(jax.random.key(seed), 6)
    return {
        "features_in": bell_draw(key_of[0], (SAMPLES, H, COLS, C), 1.0, 6.0, ((0, 4), (1, 8), (3, 16))),
        "depth_weights": bell_draw(key_of[1], (3, 3, 3, C), 9 ** -0.5, 2.0, ((3, 16),)),
        "point_weights": bell_draw(key_of[2], (4, C, F), C ** -0.5, 0.125, ((1, 16),)),
        "proj_weights": bell_draw(key_of[3], (4, F, F), (4 * F) ** -0.5, 0.1875),
        "cotangent": bell_draw(key_of[4], (SAMPLES, H, COLS, F), 3.0, 18.0, ((0, 4), (1, 8), (2, 16))),
    }


def shifted(padded, top, left, band_rows, band_cols):
    return lax.slice(padded, (top, left, 0), (top + band_rows, left + band_cols, padded.shape[2]))

def per_sample(sample_in, sample_cot, depth_weights, point_weights, proj_weights):
    band_rows, band_cols, channels = sample_in.shape
    largest_reach = 3 * BASE_DILATION
    padded = jnp.pad(sample_in, ((largest_reach, largest_reach), (largest_reach, largest_reach), (0, 0)))
    branch_maps = [sample_in]
    for branch_level in range(3):
        tap_spacing = (branch_level + 1) * BASE_DILATION
        summed = jnp.zeros((band_rows, band_cols, channels), jnp.float32)
        for row_tap in range(3):
            for col_tap in range(3):
                input_kernel_tap = shifted(padded, largest_reach + (row_tap - 1) * tap_spacing, largest_reach + (col_tap - 1) * tap_spacing, band_rows, band_cols)
                summed = summed + input_kernel_tap.astype(jnp.float32) * depth_weights[branch_level, row_tap, col_tap].astype(jnp.float32)
        branch_maps.append(summed.astype(jnp.bfloat16))
    spread = jnp.stack(branch_maps)
    point32 = point_weights.astype(jnp.float32)
    proj32 = proj_weights.astype(jnp.float32)
    preact = jnp.einsum('brwc,bcf->brwf', spread.astype(jnp.float32), point32)
    activation = jax.nn.silu(preact).astype(jnp.bfloat16)
    output = jnp.einsum('brwf,bfg->rwg', activation.astype(jnp.float32), proj32).astype(jnp.bfloat16)
    cot32 = sample_cot.astype(jnp.float32)
    silu_gradient = jnp.einsum('rwg,bfg->brwf', cot32, proj32)
    logistic = jax.nn.sigmoid(preact)
    pre_grad = (silu_gradient * logistic * (1.0 + preact * (1.0 - logistic))).astype(jnp.bfloat16)
    grad_proj = jnp.einsum('brwf,rwg->bfg', activation.astype(jnp.float32), cot32)
    spread_grad = jnp.einsum('brwf,bcf->brwc', pre_grad.astype(jnp.float32), point32).astype(jnp.bfloat16)
    grad_point = jnp.einsum('brwc,brwf->bcf', spread.astype(jnp.float32), pre_grad.astype(jnp.float32))
    grad_in = spread_grad[0].astype(jnp.float32)
    depth_rows = []
    for branch_level in range(3):
        tap_spacing = (branch_level + 1) * BASE_DILATION
        branch_grad = spread_grad[branch_level + 1]
        grad_padded = jnp.pad(branch_grad, ((largest_reach, largest_reach), (largest_reach, largest_reach), (0, 0)))
        gathered = []
        for row_tap in range(3):
            for col_tap in range(3):
                grad_tap = shifted(grad_padded, largest_reach - (row_tap - 1) * tap_spacing, largest_reach - (col_tap - 1) * tap_spacing, band_rows, band_cols)
                grad_in = grad_in + grad_tap.astype(jnp.float32) * depth_weights[branch_level, row_tap, col_tap].astype(jnp.float32)
                input_kernel_tap = shifted(padded, largest_reach + (row_tap - 1) * tap_spacing, largest_reach + (col_tap - 1) * tap_spacing, band_rows, band_cols)
                gathered.append(lax.optimization_barrier(jnp.sum(input_kernel_tap.astype(jnp.float32) * branch_grad.astype(jnp.float32), axis=(0, 1))))
        depth_rows.append(jnp.stack(gathered).reshape(3, 3, channels))
    grad_depth = jnp.stack(depth_rows)
    return (output, grad_in.astype(jnp.bfloat16), grad_depth, grad_point, grad_proj)

def reference(features_in, depth_weights, point_weights, proj_weights, cotangent):

    def apply_one(pair):
        return per_sample(pair[0], pair[1], depth_weights, point_weights, proj_weights)
    results = lax.map(apply_one, (features_in, cotangent))
    weight_scale = 1.0 / math.sqrt(SAMPLES * H * COLS)
    output = results[0]
    grad_input = results[1]
    grad_depth = lax.optimization_barrier(jnp.sum(results[2], axis=0)) * weight_scale
    grad_point = lax.optimization_barrier(jnp.sum(results[3], axis=0)) * weight_scale
    grad_proj = lax.optimization_barrier(jnp.sum(results[4], axis=0)) * weight_scale
    return (output, grad_input, grad_depth, grad_point, grad_proj)
```

```python
import functools
import math

import jax
import jax.numpy as jnp
from jax import lax
from jax.experimental import pallas as pl
from jax.experimental.pallas import tpu as pltpu
from jax.sharding import PartitionSpec as P

BASE_DILATION = 12
ROW_CLASSES = 2
COL_CLASSES = 4
MESH = pl.DeviceIdType.MESH


def reduce_kernel(rows, dps, x_ref, out_ref, landed, total, gathered, send1, recv1, send2, recv2):
    count = rows * dps
    me = lax.axis_index("row") * dps + lax.axis_index("dp")

    def device(step):
        peer = lax.rem(me + step, count)
        return peer, {"row": lax.div(peer, dps), "dp": lax.rem(peer, dps)}

    barrier = pltpu.get_barrier_semaphore()
    for step in range(1, count):
        pl.semaphore_signal(barrier, inc=1, device_id=device(step)[1], device_id_type=MESH)
    pl.semaphore_wait(barrier, count - 1)

    def scatter(step):
        peer, where = device(step)
        return pltpu.make_async_remote_copy(
            src_ref=x_ref.at[peer],
            dst_ref=landed.at[step],
            send_sem=send1.at[step],
            recv_sem=recv1.at[step],
            device_id=where,
            device_id_type=MESH,
        )

    def gather(step):
        _, where = device(step)
        return pltpu.make_async_remote_copy(
            src_ref=total,
            dst_ref=gathered.at[me],
            send_sem=send2.at[step],
            recv_sem=recv2.at[step],
            device_id=where,
            device_id_type=MESH,
        )

    for step in range(1, count):
        scatter(step).start()
    summed = x_ref[me]
    for step in range(1, count):
        scatter(step).wait_recv()
        summed = summed + landed[step]
    total[...] = summed
    for step in range(1, count):
        gather(step).start()
    for step in range(1, count):
        scatter(step).wait_send()
    for step in range(1, count):
        gather(step).wait()
    out_ref[...] = gathered[...]
    out_ref[me] = total[...]


def group_sum(value, collective_id):
    rows, dps = lax.axis_size("row"), lax.axis_size("dp")
    count, height, width = value.shape
    return pl.pallas_call(
        functools.partial(reduce_kernel, rows, dps),
        out_shape=jax.ShapeDtypeStruct(value.shape, jnp.float32),
        in_specs=[pl.BlockSpec(memory_space=pltpu.VMEM)],
        out_specs=pl.BlockSpec(memory_space=pltpu.VMEM),
        scratch_shapes=[
            pltpu.VMEM((count, height, width), jnp.float32),
            pltpu.VMEM((height, width), jnp.float32),
            pltpu.VMEM((count, height, width), jnp.float32),
            pltpu.SemaphoreType.DMA((count,)),
            pltpu.SemaphoreType.DMA((count,)),
            pltpu.SemaphoreType.DMA((count,)),
            pltpu.SemaphoreType.DMA((count,)),
        ],
        compiler_params=pltpu.CompilerParams(collective_id=collective_id, has_side_effects=True),
    )(value)


def exchange(value, axis):
    return lax.all_to_all(value, axis, split_axis=0, concat_axis=0, tiled=True)


def window(source, left, top, cols, rows):
    return source[left : left + cols, top : top + rows]


def on_device(features_in, depth_weights, point_weights, proj_weights, cotangent):
    samples, band_rows, band_cols, channels = features_in.shape
    bands, shares, dps = lax.axis_size("row"), lax.axis_size("chan"), lax.axis_size("dp")
    branches, _, width = point_weights.shape
    weight_scale = 1.0 / math.sqrt(samples * dps * band_rows * bands * band_cols)
    half = band_rows // ROW_CLASSES
    cols = band_cols // COL_CLASSES
    rows = half * bands
    row_step, col_step = BASE_DILATION // ROW_CLASSES, BASE_DILATION // COL_CLASSES

    classes = features_in.reshape(half, ROW_CLASSES, cols, COL_CLASSES, channels)
    classes = classes.transpose(1, 3, 0, 2, 4).reshape(bands, half, cols, channels)
    grid = exchange(classes, "row").reshape(rows, cols, channels).transpose(1, 0, 2)
    cells = cotangent.reshape(half, ROW_CLASSES, COL_CLASSES, width).transpose(1, 2, 0, 3)
    cot = exchange(cells.reshape(bands, half, width), "row").reshape(rows, width)
    full_point = lax.all_gather(point_weights, "chan", axis=0)
    full_cot = lax.all_gather(cot, "chan", axis=0)

    pads = ((3 * col_step, 3 * col_step), (3 * row_step, 3 * row_step), (0, 0))
    padded = jnp.pad(grid, pads)
    weights = depth_weights.astype(jnp.float32)
    maps = [grid]
    for level in range(1, branches):
        summed = jnp.zeros(grid.shape, jnp.float32)
        for i in range(3):
            for j in range(3):
                tap = window(
                    padded,
                    3 * col_step + (j - 1) * level * col_step,
                    3 * row_step + (i - 1) * level * row_step,
                    cols,
                    rows,
                )
                summed = summed + tap.astype(jnp.float32) * weights[level - 1, i, j]
        maps.append(summed.astype(jnp.bfloat16))
    spread = jnp.stack(maps, axis=1)
    preact = jnp.einsum(
        "gbnk,gbkf->bnf",
        exchange(spread, "chan"),
        full_point,
        preferred_element_type=jnp.float32,
    )
    logistic = jax.nn.sigmoid(preact)
    activation = (preact * logistic).astype(jnp.bfloat16)
    act_grad = jnp.einsum("ng,bfg->bnf", cot, proj_weights, preferred_element_type=jnp.float32)
    pre_grad = (act_grad * logistic * (1.0 + preact * (1.0 - logistic))).astype(jnp.bfloat16)
    incoming = lax.all_gather(pre_grad, "chan", axis=0)

    out_cells = jnp.einsum(
        "bnf,bfg->ng", activation, proj_weights, preferred_element_type=jnp.float32
    ).astype(jnp.bfloat16)
    output = exchange(out_cells.reshape(bands, half, width), "row")
    output = output.reshape(ROW_CLASSES, COL_CLASSES, half, width).transpose(2, 0, 1, 3)
    output = output.reshape(1, band_rows, COL_CLASSES, width)

    slices = shares // branches
    part = width // slices
    packed = activation.reshape(branches, 2, rows // 2, slices, part)
    packed = packed.transpose(0, 3, 2, 1, 4).reshape(shares, rows // 2, 2 * part)
    packed = exchange(packed, "chan")
    proj_part = jnp.zeros((part, width), jnp.float32)
    for side in range(2):
        proj_part = proj_part + jnp.einsum(
            "xnf,xng->fg",
            packed[:, :, side * part : (side + 1) * part],
            full_cot[:, side * (rows // 2) : (side + 1) * (rows // 2)],
            preferred_element_type=jnp.float32,
        )
    group = bands * dps
    proj_part = group_sum(proj_part.reshape(group, part // group, width), 0)
    proj_part = proj_part.reshape(part, width) * weight_scale
    grad_proj = lax.all_gather(proj_part, "chan", axis=0).reshape(branches, width, width)

    point_sum = jnp.einsum("xbnk,xbnf->bkf", spread, incoming, preferred_element_type=jnp.float32)
    spread_grad = jnp.einsum(
        "xbnf,bkf->bxnk", incoming, point_weights, preferred_element_type=jnp.float32
    ).astype(jnp.bfloat16)
    grad_in = spread_grad[0].astype(jnp.float32)
    depth_sums = []
    for level in range(1, branches):
        branch_grad = spread_grad[level].astype(jnp.float32)
        grad_padded = jnp.pad(spread_grad[level], pads)
        for i in range(3):
            for j in range(3):
                left, top = (j - 1) * level * col_step, (i - 1) * level * row_step
                tap = window(padded, 3 * col_step + left, 3 * row_step + top, cols, rows)
                depth_sums.append(jnp.sum(tap.astype(jnp.float32) * branch_grad, axis=(0, 1)))
                grad_tap = window(
                    grad_padded, 3 * col_step - left, 3 * row_step - top, cols, rows
                )
                grad_in = grad_in + grad_tap.astype(jnp.float32) * weights[level - 1, i, j]
    returned = grad_in.astype(jnp.bfloat16).transpose(1, 0, 2)
    returned = exchange(returned.reshape(bands, half, cols, channels), "row")
    returned = returned.reshape(ROW_CLASSES, COL_CLASSES, half, cols, channels)
    grad_input = returned.transpose(2, 0, 3, 1, 4).reshape(features_in.shape)

    taps = len(depth_sums)
    depth_part = jnp.pad(jnp.stack(depth_sums), ((0, group - taps), (0, width - channels)))
    summed = group_sum(
        jnp.concatenate(
            [
                point_sum.reshape(group, branches * channels // group, width),
                depth_part[:, None],
            ],
            axis=1,
        ),
        1,
    )
    grad_point = summed[:, :-1].reshape(point_weights.shape) * weight_scale
    grad_depth = summed[:taps, -1, :channels].reshape(depth_weights.shape) * weight_scale
    return (output, grad_input, grad_depth, grad_point, grad_proj)


def solution(mesh):
    in_specs = (
        P("dp", "row", None, "chan"),
        P(None, None, None, "chan"),
        P(None, "chan", None),
        P(),
        P("dp", "row", "chan", None),
    )
    out_specs = (
        P("dp", "row", "chan", None),
        P("dp", "row", None, "chan"),
        P(None, None, None, "chan"),
        P(None, "chan", None),
        P(),
    )
    return jax.shard_map(
        on_device, mesh=mesh, in_specs=in_specs, out_specs=out_specs, check_vma=False
    )
```

```python
import functools
import math

import jax
import jax.numpy as jnp
from jax import lax
from jax.experimental import pallas as pl
from jax.experimental.pallas import tpu as pltpu
from jax.sharding import PartitionSpec as P

BASE_DILATION = 12
ROW_CLASSES = 2
COL_CLASSES = 4
MESH = pl.DeviceIdType.MESH


def reduce_kernel(rows, dps, x_ref, out_ref, landed, total, gathered, send1, recv1, send2, recv2):
    count = rows * dps
    me = lax.axis_index("row") * dps + lax.axis_index("dp")

    def device(step):
        peer = lax.rem(me + step, count)
        return peer, {"row": lax.div(peer, dps), "dp": lax.rem(peer, dps)}

    barrier = pltpu.get_barrier_semaphore()
    for step in range(1, count):
        pl.semaphore_signal(barrier, inc=1, device_id=device(step)[1], device_id_type=MESH)
    pl.semaphore_wait(barrier, count - 1)

    def scatter(step):
        peer, where = device(step)
        return pltpu.make_async_remote_copy(
            src_ref=x_ref.at[peer],
            dst_ref=landed.at[step],
            send_sem=send1.at[step],
            recv_sem=recv1.at[step],
            device_id=where,
            device_id_type=MESH,
        )

    def gather(step):
        _, where = device(step)
        return pltpu.make_async_remote_copy(
            src_ref=total,
            dst_ref=gathered.at[me],
            send_sem=send2.at[step],
            recv_sem=recv2.at[step],
            device_id=where,
            device_id_type=MESH,
        )

    for step in range(1, count):
        scatter(step).start()
    summed = x_ref[me].astype(jnp.float32)
    for step in range(1, count):
        scatter(step).wait_recv()
        summed = summed + landed[step].astype(jnp.float32)
    total[...] = summed.astype(total.dtype)
    for step in range(1, count):
        gather(step).start()
    for step in range(1, count):
        scatter(step).wait_send()
    for step in range(1, count):
        gather(step).wait()
    out_ref[...] = gathered[...]
    out_ref[me] = total[...]


def group_sum(value, collective_id):
    rows, dps = lax.axis_size("row"), lax.axis_size("dp")
    count, height, width = value.shape
    return pl.pallas_call(
        functools.partial(reduce_kernel, rows, dps),
        out_shape=jax.ShapeDtypeStruct(value.shape, value.dtype),
        in_specs=[pl.BlockSpec(memory_space=pltpu.VMEM)],
        out_specs=pl.BlockSpec(memory_space=pltpu.VMEM),
        scratch_shapes=[
            pltpu.VMEM((count, height, width), value.dtype),
            pltpu.VMEM((height, width), value.dtype),
            pltpu.VMEM((count, height, width), value.dtype),
            pltpu.SemaphoreType.DMA((count,)),
            pltpu.SemaphoreType.DMA((count,)),
            pltpu.SemaphoreType.DMA((count,)),
            pltpu.SemaphoreType.DMA((count,)),
        ],
        compiler_params=pltpu.CompilerParams(collective_id=collective_id, has_side_effects=True),
        cost_estimate=pl.CostEstimate(flops=0, bytes_accessed=80_000_000, transcendentals=0),
    )(value)


def ring_kernel(chips, cut, x_ref, out_ref, held, ring_send, ring_recv, pair_send, pair_recv):
    me = lax.axis_index("chan")
    chip, core = lax.div(me, 2), lax.rem(me, 2)
    hops = chips // 2
    size = x_ref.shape[0]
    spans = (pl.ds(0, cut), pl.ds(cut, size - cut))

    def block(away):
        return lax.rem(chip + away + chips, chips) * 2 + core

    ahead = {"chan": block(1)}
    behind = {"chan": block(-1)}
    twin = {"chan": chip * 2 + 1 - core}
    targets = (ahead, behind)

    barrier = pltpu.get_barrier_semaphore()
    for where in (ahead, behind, twin):
        pl.semaphore_signal(barrier, inc=1, device_id=where, device_id_type=MESH)
    pl.semaphore_wait(barrier, 3)

    def ring(way, hop):
        away = 1 - hop if way == 0 else hop - 1
        source, landing = (x_ref if hop == 1 else held.at[block(away)]), held.at[block(away)]
        if hop == hops:
            source, landing = source.at[spans[way]], landing.at[spans[way]]
        return pltpu.make_async_remote_copy(
            src_ref=source,
            dst_ref=landing,
            send_sem=ring_send.at[way, hop],
            recv_sem=ring_recv.at[way, hop],
            device_id=targets[way],
            device_id_type=MESH,
        )

    def pair(way, hop):
        away = -hop if way == 0 else hop
        source, landing = (x_ref if hop == 0 else held.at[block(away)]), held.at[block(away)]
        if hop == hops:
            source, landing = source.at[spans[way]], landing.at[spans[way]]
        return pltpu.make_async_remote_copy(
            src_ref=source,
            dst_ref=landing,
            send_sem=pair_send.at[way, hop],
            recv_sem=pair_recv.at[way, hop],
            device_id=twin,
            device_id_type=MESH,
        )

    pairs = [(0, 0)]
    for way in range(2):
        ring(way, 1).start()
    pair(0, 0).start()
    for hop in range(1, hops + 1):
        for way in range(2):
            ring(way, hop).wait_recv()
            if hop < hops:
                ring(way, hop + 1).start()
            pair(way, hop).start()
            pairs.append((way, hop))
    for hop in range(1, hops + 1):
        for way in range(2):
            ring(way, hop).wait_send()
    for way, hop in pairs:
        pair(way, hop).wait()
    out_ref[...] = held[...]
    out_ref[me] = x_ref[...]


def ring_gather(value, cut, collective_id):
    shares = lax.axis_size("chan")
    chips = shares // 2
    sems = pltpu.SemaphoreType.DMA((2, chips // 2 + 1))
    return pl.pallas_call(
        functools.partial(ring_kernel, chips, cut),
        out_shape=jax.ShapeDtypeStruct((shares,) + value.shape, value.dtype),
        in_specs=[pl.BlockSpec(memory_space=pltpu.VMEM)],
        out_specs=pl.BlockSpec(memory_space=pltpu.VMEM),
        scratch_shapes=[
            pltpu.VMEM((shares,) + value.shape, value.dtype), sems, sems, sems, sems
        ],
        compiler_params=pltpu.CompilerParams(collective_id=collective_id, has_side_effects=True),
        cost_estimate=pl.CostEstimate(flops=0, bytes_accessed=80_000_000, transcendentals=0),
    )(value)


def exchange(value, axis):
    return lax.all_to_all(value, axis, split_axis=0, concat_axis=0, tiled=True)


def window(source, left, top, cols, rows):
    return source[left : left + cols, top : top + rows]


def on_device(features_in, depth_weights, point_weights, proj_weights, cotangent):
    samples, band_rows, band_cols, channels = features_in.shape
    bands, shares, dps = lax.axis_size("row"), lax.axis_size("chan"), lax.axis_size("dp")
    branches, _, width = point_weights.shape
    weight_scale = 1.0 / math.sqrt(samples * dps * band_rows * bands * band_cols)
    half = band_rows // ROW_CLASSES
    cols = band_cols // COL_CLASSES
    rows = half * bands
    row_step, col_step = BASE_DILATION // ROW_CLASSES, BASE_DILATION // COL_CLASSES

    classes = features_in.reshape(half, ROW_CLASSES, cols, COL_CLASSES, channels)
    classes = classes.transpose(1, 3, 0, 2, 4).reshape(bands, half * cols, channels)
    cells = cotangent.reshape(half, ROW_CLASSES, COL_CLASSES, width).transpose(1, 2, 0, 3)
    cells = cells.reshape(bands, half, width)
    landed = exchange(
        jnp.concatenate([classes, cells[:, :, :channels], cells[:, :, channels:]], axis=1), "row"
    )
    area = half * cols
    grid = landed[:, :area].reshape(rows, cols, channels).transpose(1, 0, 2)
    cot = jnp.concatenate([landed[:, area : area + half], landed[:, area + half :]], axis=2)
    cot = cot.reshape(rows, width)
    full_point = lax.all_gather(point_weights, "chan", axis=0)

    pads = ((3 * col_step, 3 * col_step), (3 * row_step, 3 * row_step), (0, 0))
    padded = jnp.pad(grid, pads)
    weights = depth_weights.astype(jnp.float32)
    maps = [grid]
    for level in range(1, branches):
        summed = jnp.zeros(grid.shape, jnp.float32)
        for i in range(3):
            for j in range(3):
                tap = window(
                    padded,
                    3 * col_step + (j - 1) * level * col_step,
                    3 * row_step + (i - 1) * level * row_step,
                    cols,
                    rows,
                )
                summed = summed + tap.astype(jnp.float32) * weights[level - 1, i, j]
        maps.append(summed.astype(jnp.bfloat16))
    spread = jnp.stack(maps, axis=1)
    preact = jnp.einsum(
        "gbnk,gbkf->bnf",
        exchange(spread, "chan"),
        full_point,
        preferred_element_type=jnp.float32,
    )
    logistic = jax.nn.sigmoid(preact)
    activation = (preact * logistic).astype(jnp.bfloat16)
    act_grad = jnp.einsum("ng,bfg->bnf", cot, proj_weights, preferred_element_type=jnp.float32)
    pre_grad = (act_grad * logistic * (1.0 + preact * (1.0 - logistic))).astype(jnp.bfloat16)
    out_cells = jnp.einsum(
        "bnf,bfg->ng", activation, proj_weights, preferred_element_type=jnp.float32
    ).astype(jnp.bfloat16)

    slices = shares // branches
    part = width // slices
    packed = activation.reshape(branches, 2, rows // 2, slices, part)
    packed = packed.transpose(0, 3, 2, 1, 4).reshape(shares, rows // 2, 2 * part)
    packed = exchange(packed, "chan")
    sent = jnp.concatenate([pre_grad.reshape(branches * rows, width), cot], axis=0)
    held = ring_gather(sent, sent.shape[0] // 32 * 16, 0)
    incoming = held[:, : branches * rows].reshape(shares, branches, rows, width)
    full_cot = held[:, branches * rows :]
    proj_part = jnp.zeros((part, width), jnp.float32)
    for side in range(2):
        proj_part = proj_part + jnp.einsum(
            "xnf,xng->fg",
            packed[:, :, side * part : (side + 1) * part],
            full_cot[:, side * (rows // 2) : (side + 1) * (rows // 2)],
            preferred_element_type=jnp.float32,
        )
    group = bands * dps
    point_sum = jnp.einsum("xbnk,xbnf->bkf", spread, incoming, preferred_element_type=jnp.float32)
    spread_grad = jnp.einsum(
        "xbnf,bkf->bxnk", incoming, point_weights, preferred_element_type=jnp.float32
    ).astype(jnp.bfloat16)
    grad_in = spread_grad[0].astype(jnp.float32)
    depth_sums = []
    for level in range(1, branches):
        branch_grad = spread_grad[level].astype(jnp.float32)
        grad_padded = jnp.pad(spread_grad[level], pads)
        for i in range(3):
            for j in range(3):
                left, top = (j - 1) * level * col_step, (i - 1) * level * row_step
                tap = window(padded, 3 * col_step + left, 3 * row_step + top, cols, rows)
                depth_sums.append(jnp.sum(tap.astype(jnp.float32) * branch_grad, axis=(0, 1)))
                grad_tap = window(
                    grad_padded, 3 * col_step - left, 3 * row_step - top, cols, rows
                )
                grad_in = grad_in + grad_tap.astype(jnp.float32) * weights[level - 1, i, j]
    returned = grad_in.astype(jnp.bfloat16).transpose(1, 0, 2).reshape(bands, area, channels)
    out_cells = out_cells.reshape(bands, half, width)
    returned = exchange(
        jnp.concatenate([returned, out_cells[:, :, :channels], out_cells[:, :, channels:]], axis=1),
        "row",
    )
    output = jnp.concatenate(
        [returned[:, area : area + half], returned[:, area + half :]], axis=2
    )
    output = output.reshape(ROW_CLASSES, COL_CLASSES, half, width).transpose(2, 0, 1, 3)
    output = output.reshape(1, band_rows, COL_CLASSES, width)
    grad_input = returned[:, :area].reshape(ROW_CLASSES, COL_CLASSES, half, cols, channels)
    grad_input = grad_input.transpose(2, 0, 3, 1, 4).reshape(features_in.shape)

    taps = len(depth_sums)
    depth_part = jnp.pad(jnp.stack(depth_sums), ((0, group - taps), (0, width - channels)))
    height = branches * channels // group
    summed = group_sum(
        jnp.concatenate(
            [
                point_sum.reshape(group, height, width),
                depth_part[:, None],
                proj_part.reshape(group, part // group, width),
            ],
            axis=1,
        ).astype(jnp.bfloat16),
        1,
    )
    grad_point = summed[:, :height].reshape(point_weights.shape).astype(jnp.float32) * weight_scale
    grad_depth = summed[:taps, height, :channels].reshape(depth_weights.shape)
    grad_depth = grad_depth.astype(jnp.float32) * weight_scale
    grad_proj = ring_gather(summed[:, height + 1 :].reshape(part, width), part // 2, 2)
    grad_proj = grad_proj.reshape(branches, width, width).astype(jnp.float32) * weight_scale
    return (output, grad_input, grad_depth, grad_point, grad_proj)


def solution(mesh):
    in_specs = (
        P("dp", "row", None, "chan"),
        P(None, None, None, "chan"),
        P(None, "chan", None),
        P(),
        P("dp", "row", "chan", None),
    )
    out_specs = (
        P("dp", "row", "chan", None),
        P("dp", "row", None, "chan"),
        P(None, None, None, "chan"),
        P(None, "chan", None),
        P(),
    )
    return jax.shard_map(
        on_device, mesh=mesh, in_specs=in_specs, out_specs=out_specs, check_vma=False
    )
```

```python
import functools
import math

import jax
import jax.numpy as jnp
from jax import lax
from jax.experimental import pallas as pl
from jax.experimental.pallas import tpu as pltpu
from jax.sharding import PartitionSpec as P

BASE_DILATION = 12
ROW_CLASSES = 2
COL_CLASSES = 4
MESH = pl.DeviceIdType.MESH


def reduce_kernel(rows, dps, x_ref, out_ref, land1, part, land2, total, held, send, recv):
    row, dp = lax.axis_index("row"), lax.axis_index("dp")

    def dp_peer(step):
        return lax.rem(dp + step, dps)

    def row_peer(step):
        return lax.rem(row + step, rows)

    barrier = pltpu.get_barrier_semaphore()
    for step in range(1, dps):
        where = {"dp": dp_peer(step)}
        pl.semaphore_signal(barrier, inc=1, device_id=where, device_id_type=MESH)
    for step in range(1, rows):
        where = {"row": row_peer(step)}
        pl.semaphore_signal(barrier, inc=1, device_id=where, device_id_type=MESH)
    pl.semaphore_wait(barrier, rows + dps - 2)

    def copy(level, step):
        if level == 0:
            where, source, landing = {"dp": dp_peer(step)}, x_ref.at[dp_peer(step)], land1.at[step]
        elif level == 1:
            where, source, landing = {"row": row_peer(step)}, part.at[row_peer(step)], land2.at[step]
        elif level == 2:
            where, source, landing = {"row": row_peer(step)}, total, held.at[dp, row]
        else:
            where, source, landing = {"dp": dp_peer(step)}, held.at[dp], held.at[dp]
        return pltpu.make_async_remote_copy(
            src_ref=source,
            dst_ref=landing,
            send_sem=send.at[level, step],
            recv_sem=recv.at[level, step],
            device_id=where,
            device_id_type=MESH,
        )

    for step in range(1, dps):
        copy(0, step).start()
    summed = x_ref[dp].astype(jnp.float32)
    for step in range(1, dps):
        copy(0, step).wait_recv()
        summed = summed + land1[step].astype(jnp.float32)
    part[...] = summed.astype(part.dtype)
    for step in range(1, rows):
        copy(1, step).start()
    summed = part[row].astype(jnp.float32)
    for step in range(1, rows):
        copy(1, step).wait_recv()
        summed = summed + land2[step].astype(jnp.float32)
    total[...] = summed.astype(total.dtype)
    held[dp, row] = total[...]
    for step in range(1, rows):
        copy(2, step).start()
    for step in range(1, rows):
        copy(2, step).wait_recv()
    for step in range(1, dps):
        copy(3, step).start()
    for step in range(1, dps):
        copy(0, step).wait_send()
    for level in (1, 2):
        for step in range(1, rows):
            copy(level, step).wait_send()
    for step in range(1, dps):
        copy(3, step).wait()
    out_ref[...] = held[...]


def group_sum(value, collective_id):
    dps, rows, height, width = value.shape
    sems = pltpu.SemaphoreType.DMA((4, max(rows, dps)))
    return pl.pallas_call(
        functools.partial(reduce_kernel, rows, dps),
        out_shape=jax.ShapeDtypeStruct(value.shape, value.dtype),
        in_specs=[pl.BlockSpec(memory_space=pltpu.VMEM)],
        out_specs=pl.BlockSpec(memory_space=pltpu.VMEM),
        scratch_shapes=[
            pltpu.VMEM(value.shape, value.dtype),
            pltpu.VMEM((rows, height, width), value.dtype),
            pltpu.VMEM((rows, height, width), value.dtype),
            pltpu.VMEM((height, width), value.dtype),
            pltpu.VMEM(value.shape, value.dtype),
            sems,
            sems,
        ],
        compiler_params=pltpu.CompilerParams(collective_id=collective_id, has_side_effects=True),
        cost_estimate=pl.CostEstimate(flops=0, bytes_accessed=80_000_000, transcendentals=0),
    )(value)


def ring_kernel(chips, cut, deal, *refs):
    if deal:
        x_ref, y_ref, out_ref, dealt_ref, held, dealt = refs[:6]
        deal_send, deal_recv, twin_send, twin_recv = refs[6:10]
    else:
        x_ref, out_ref, held = refs[:3]
    ring_send, ring_recv, pair_send, pair_recv = refs[-4:]
    me = lax.axis_index("chan")
    chip, core = lax.div(me, 2), lax.rem(me, 2)
    hops = chips // 2
    size = x_ref.shape[0]
    spans = (pl.ds(0, cut), pl.ds(cut, size - cut))

    def block(away):
        return lax.rem(chip + away + chips, chips) * 2 + core

    ahead = {"chan": block(1)}
    behind = {"chan": block(-1)}
    twin = {"chan": chip * 2 + 1 - core}
    targets = (ahead, behind)

    barrier = pltpu.get_barrier_semaphore()
    greeted = [twin]
    if deal:
        greeted += [{"chan": block(step)} for step in range(1, chips)]
    else:
        greeted += [ahead, behind]
    for where in greeted:
        pl.semaphore_signal(barrier, inc=1, device_id=where, device_id_type=MESH)
    pl.semaphore_wait(barrier, len(greeted))

    def direct(step):
        return pltpu.make_async_remote_copy(
            src_ref=y_ref.at[lax.rem(chip + step, chips)],
            dst_ref=dealt.at[me],
            send_sem=deal_send.at[step],
            recv_sem=deal_recv.at[step],
            device_id={"chan": block(step)},
            device_id_type=MESH,
        )

    def onward(step):
        slot = block(-step)
        return pltpu.make_async_remote_copy(
            src_ref=y_ref.at[chip] if step == 0 else dealt.at[slot],
            dst_ref=dealt.at[slot],
            send_sem=twin_send.at[step],
            recv_sem=twin_recv.at[step],
            device_id=twin,
            device_id_type=MESH,
        )

    def ring(way, hop):
        away = 1 - hop if way == 0 else hop - 1
        source, landing = (x_ref if hop == 1 else held.at[block(away)]), held.at[block(away)]
        if hop == hops:
            source, landing = source.at[spans[way]], landing.at[spans[way]]
        return pltpu.make_async_remote_copy(
            src_ref=source,
            dst_ref=landing,
            send_sem=ring_send.at[way, hop],
            recv_sem=ring_recv.at[way, hop],
            device_id=targets[way],
            device_id_type=MESH,
        )

    def pair(way, hop):
        away = -hop if way == 0 else hop
        source, landing = (x_ref if hop == 0 else held.at[block(away)]), held.at[block(away)]
        if hop == hops:
            source, landing = source.at[spans[way]], landing.at[spans[way]]
        return pltpu.make_async_remote_copy(
            src_ref=source,
            dst_ref=landing,
            send_sem=pair_send.at[way, hop],
            recv_sem=pair_recv.at[way, hop],
            device_id=twin,
            device_id_type=MESH,
        )

    pairs = [(0, 0)]
    for way in range(2):
        ring(way, 1).start()
    pair(0, 0).start()
    if deal:
        for step in range(1, chips):
            direct(step).start()
        onward(0).start()
    for hop in range(1, hops + 1):
        if deal and hop == hops:
            for step in range(1, chips):
                direct(step).wait_recv()
                onward(step).start()
        for way in range(2):
            ring(way, hop).wait_recv()
            if hop < hops:
                ring(way, hop + 1).start()
            pair(way, hop).start()
            pairs.append((way, hop))
    for hop in range(1, hops + 1):
        for way in range(2):
            ring(way, hop).wait_send()
    for way, hop in pairs:
        pair(way, hop).wait()
    out_ref[...] = held[...]
    out_ref[me] = x_ref[...]
    if deal:
        for step in range(1, chips):
            direct(step).wait_send()
        for step in range(chips):
            onward(step).wait()
        dealt_ref[...] = dealt[...]
        dealt_ref[me] = y_ref[chip]


def ring_gather(value, cut, collective_id, dealt=None):
    shares = lax.axis_size("chan")
    chips = shares // 2
    operands = [value] if dealt is None else [value, dealt]
    gathered = [(shares,) + value.shape]
    if dealt is not None:
        gathered.append((shares,) + dealt.shape[1:])
    scratch = [pltpu.VMEM(shape, value.dtype) for shape in gathered]
    if dealt is not None:
        scratch += [pltpu.SemaphoreType.DMA((chips,))] * 4
    scratch += [pltpu.SemaphoreType.DMA((2, chips // 2 + 1))] * 4
    vmem = pl.BlockSpec(memory_space=pltpu.VMEM)
    result = pl.pallas_call(
        functools.partial(ring_kernel, chips, cut, dealt is not None),
        out_shape=[jax.ShapeDtypeStruct(shape, value.dtype) for shape in gathered],
        in_specs=[vmem] * len(operands),
        out_specs=[vmem] * len(gathered),
        scratch_shapes=scratch,
        compiler_params=pltpu.CompilerParams(collective_id=collective_id, has_side_effects=True),
        cost_estimate=pl.CostEstimate(flops=0, bytes_accessed=80_000_000, transcendentals=0),
    )(*operands)
    return result[0] if dealt is None else result


def exchange(value, axis):
    return lax.all_to_all(value, axis, split_axis=0, concat_axis=0, tiled=True)


def window(source, left, top, cols, rows):
    return source[left : left + cols, top : top + rows]


def on_device(features_in, depth_weights, point_weights, proj_weights, cotangent):
    samples, band_rows, band_cols, channels = features_in.shape
    bands, shares, dps = lax.axis_size("row"), lax.axis_size("chan"), lax.axis_size("dp")
    branches, _, width = point_weights.shape
    weight_scale = 1.0 / math.sqrt(samples * dps * band_rows * bands * band_cols)
    half = band_rows // ROW_CLASSES
    cols = band_cols // COL_CLASSES
    rows = half * bands
    row_step, col_step = BASE_DILATION // ROW_CLASSES, BASE_DILATION // COL_CLASSES

    classes = features_in.reshape(half, ROW_CLASSES, cols, COL_CLASSES, channels)
    classes = classes.transpose(1, 3, 0, 2, 4).reshape(bands, half * cols, channels)
    cells = cotangent.reshape(half, ROW_CLASSES, COL_CLASSES, width).transpose(1, 2, 0, 3)
    cells = cells.reshape(bands, half, width)
    landed = exchange(
        jnp.concatenate([classes, cells[:, :, :channels], cells[:, :, channels:]], axis=1), "row"
    )
    area = half * cols
    grid = landed[:, :area].reshape(rows, cols, channels).transpose(1, 0, 2)
    cot = jnp.concatenate([landed[:, area : area + half], landed[:, area + half :]], axis=2)
    cot = cot.reshape(rows, width)
    full_point = ring_gather(
        point_weights.reshape(branches * channels, width), branches * channels // 2, 3
    ).reshape((shares,) + point_weights.shape)

    pads = ((3 * col_step, 3 * col_step), (3 * row_step, 3 * row_step), (0, 0))
    padded = jnp.pad(grid, pads)
    weights = depth_weights.astype(jnp.float32)
    maps = [grid]
    for level in range(1, branches):
        summed = jnp.zeros(grid.shape, jnp.float32)
        for i in range(3):
            for j in range(3):
                tap = window(
                    padded,
                    3 * col_step + (j - 1) * level * col_step,
                    3 * row_step + (i - 1) * level * row_step,
                    cols,
                    rows,
                )
                summed = summed + tap.astype(jnp.float32) * weights[level - 1, i, j]
        maps.append(summed.astype(jnp.bfloat16))
    spread = jnp.stack(maps, axis=1)
    preact = jnp.einsum(
        "gbnk,gbkf->bnf",
        exchange(spread, "chan"),
        full_point,
        preferred_element_type=jnp.float32,
    )
    logistic = jax.nn.sigmoid(preact)
    activation = (preact * logistic).astype(jnp.bfloat16)
    act_grad = jnp.einsum("ng,bfg->bnf", cot, proj_weights, preferred_element_type=jnp.float32)
    pre_grad = (act_grad * logistic * (1.0 + preact * (1.0 - logistic))).astype(jnp.bfloat16)
    out_cells = jnp.einsum(
        "bnf,bfg->ng", activation, proj_weights, preferred_element_type=jnp.float32
    ).astype(jnp.bfloat16)

    chips = shares // 2
    per = chips // branches
    part, side = width // per, width // 2
    pieces = activation.reshape(branches, rows, per, part).transpose(0, 2, 1, 3)
    sent = jnp.concatenate([pre_grad.reshape(branches * rows, width), cot], axis=0)
    held, slices = ring_gather(
        sent, sent.shape[0] // 32 * 16, 0, pieces.reshape(chips, rows, part)
    )
    incoming = held[:, : branches * rows].reshape(shares, branches, rows, width)
    core = lax.rem(lax.axis_index("chan"), 2)
    cot_side = lax.dynamic_slice_in_dim(held[:, branches * rows :], core * side, side, axis=2)
    proj_part = jnp.einsum(
        "xnf,xng->fg", slices, cot_side, preferred_element_type=jnp.float32
    )
    proj_part = jnp.concatenate([proj_part[: part // 2], proj_part[part // 2 :]], axis=1)
    group = bands * dps
    point_sum = jnp.einsum("xbnk,xbnf->bkf", spread, incoming, preferred_element_type=jnp.float32)
    spread_grad = jnp.einsum(
        "xbnf,bkf->bxnk", incoming, point_weights, preferred_element_type=jnp.float32
    ).astype(jnp.bfloat16)
    grad_in = spread_grad[0].astype(jnp.float32)
    depth_sums = []
    for level in range(1, branches):
        branch_grad = spread_grad[level].astype(jnp.float32)
        grad_padded = jnp.pad(spread_grad[level], pads)
        for i in range(3):
            for j in range(3):
                left, top = (j - 1) * level * col_step, (i - 1) * level * row_step
                tap = window(padded, 3 * col_step + left, 3 * row_step + top, cols, rows)
                depth_sums.append(jnp.sum(tap.astype(jnp.float32) * branch_grad, axis=(0, 1)))
                grad_tap = window(
                    grad_padded, 3 * col_step - left, 3 * row_step - top, cols, rows
                )
                grad_in = grad_in + grad_tap.astype(jnp.float32) * weights[level - 1, i, j]
    returned = grad_in.astype(jnp.bfloat16).transpose(1, 0, 2).reshape(bands, area, channels)
    out_cells = out_cells.reshape(bands, half, width)
    returned = exchange(
        jnp.concatenate([returned, out_cells[:, :, :channels], out_cells[:, :, channels:]], axis=1),
        "row",
    )
    output = jnp.concatenate(
        [returned[:, area : area + half], returned[:, area + half :]], axis=2
    )
    output = output.reshape(ROW_CLASSES, COL_CLASSES, half, width).transpose(2, 0, 1, 3)
    output = output.reshape(1, band_rows, COL_CLASSES, width)
    grad_input = returned[:, :area].reshape(ROW_CLASSES, COL_CLASSES, half, cols, channels)
    grad_input = grad_input.transpose(2, 0, 3, 1, 4).reshape(features_in.shape)

    taps = len(depth_sums)
    depth_part = jnp.pad(jnp.stack(depth_sums), ((0, group - taps), (0, width - channels)))
    height = branches * channels // group
    summed = group_sum(
        jnp.concatenate(
            [
                point_sum.reshape(group, height, width),
                depth_part[:, None],
                proj_part.reshape(group, part // 2 // group, width),
            ],
            axis=1,
        )
        .astype(jnp.bfloat16)
        .reshape(dps, bands, -1, width),
        1,
    ).reshape(group, -1, width)
    grad_point = summed[:, :height].reshape(point_weights.shape).astype(jnp.float32) * weight_scale
    grad_depth = summed[:taps, height, :channels].reshape(depth_weights.shape)
    grad_depth = grad_depth.astype(jnp.float32) * weight_scale
    grad_proj = ring_gather(summed[:, height + 1 :].reshape(part // 2, width), part // 4, 2)
    grad_proj = grad_proj.reshape(branches, per, 2, part // 2, 2, side).transpose(0, 1, 4, 3, 2, 5)
    grad_proj = grad_proj.reshape(branches, width, width).astype(jnp.float32) * weight_scale
    return (output, grad_input, grad_depth, grad_point, grad_proj)


def solution(mesh):
    in_specs = (
        P("dp", "row", None, "chan"),
        P(None, None, None, "chan"),
        P(None, "chan", None),
        P(),
        P("dp", "row", "chan", None),
    )
    out_specs = (
        P("dp", "row", "chan", None),
        P("dp", "row", None, "chan"),
        P(None, None, None, "chan"),
        P(None, "chan", None),
        P(),
    )
    return jax.shard_map(
        on_device, mesh=mesh, in_specs=in_specs, out_specs=out_specs, check_vma=False
    )
```

```python
import functools
import math

import jax
import jax.numpy as jnp
from jax import lax
from jax.experimental import pallas as pl
from jax.experimental.pallas import tpu as pltpu
from jax.sharding import PartitionSpec as P

BASE_DILATION = 12
ROW_CLASSES = 2
COL_CLASSES = 4
MESH = pl.DeviceIdType.MESH


def remote(source, landing, send_sem, recv_sem, where):
    return pltpu.make_async_remote_copy(
        src_ref=source,
        dst_ref=landing,
        send_sem=send_sem,
        recv_sem=recv_sem,
        device_id=where,
        device_id_type=MESH,
    )


def greet(places):
    barrier = pltpu.get_barrier_semaphore()
    for where in places:
        pl.semaphore_signal(barrier, inc=1, device_id=where, device_id_type=MESH)
    pl.semaphore_wait(barrier, len(places))


class Levels:
    def __init__(self, rows, dps, x_ref, land1, part, land2, total, held, send, recv):
        self.rows, self.dps, self.x_ref = rows, dps, x_ref
        self.land1, self.part, self.land2, self.total, self.held = land1, part, land2, total, held
        self.send, self.recv = send, recv
        self.row, self.dp = lax.axis_index("row"), lax.axis_index("dp")

    def dp_peer(self, step):
        return lax.rem(self.dp + step, self.dps)

    def row_peer(self, step):
        return lax.rem(self.row + step, self.rows)

    def places(self):
        found = [{"dp": self.dp_peer(step)} for step in range(1, self.dps)]
        return found + [{"row": self.row_peer(step)} for step in range(1, self.rows)]

    def steps(self, level):
        return range(1, self.dps if level in (0, 3) else self.rows)

    def copy(self, level, step):
        if level in (0, 3):
            peer, where = self.dp_peer(step), {"dp": self.dp_peer(step)}
        else:
            peer, where = self.row_peer(step), {"row": self.row_peer(step)}
        source, landing = (
            lambda: (self.x_ref.at[peer], self.land1.at[step]),
            lambda: (self.part.at[peer], self.land2.at[step]),
            lambda: (self.total, self.held.at[self.dp, self.row]),
            lambda: (self.held.at[self.dp], self.held.at[self.dp]),
        )[level]()
        return remote(source, landing, self.send.at[level, step], self.recv.at[level, step], where)

    def start(self, level):
        for step in self.steps(level):
            self.copy(level, step).start()

    def arrive(self, level):
        if level == 0:
            summed = self.x_ref[self.dp].astype(jnp.float32)
        elif level == 1:
            summed = self.part[self.row].astype(jnp.float32)
        for step in self.steps(level):
            self.copy(level, step).wait_recv()
            if level == 0:
                summed = summed + self.land1[step].astype(jnp.float32)
            elif level == 1:
                summed = summed + self.land2[step].astype(jnp.float32)
        if level == 0:
            self.part[...] = summed.astype(self.part.dtype)
        elif level == 1:
            self.total[...] = summed.astype(self.total.dtype)
            self.held[self.dp, self.row] = self.total[...]
        if level < 3:
            self.start(level + 1)

    def finish(self):
        for level in range(4):
            for step in self.steps(level):
                self.copy(level, step).wait_send()


class Ring:
    def __init__(self, chips, cut, x_ref, held, ring_send, ring_recv, pair_send, pair_recv):
        self.chips, self.hops, self.x_ref, self.held = chips, chips // 2, x_ref, held
        self.sems = ring_send, ring_recv, pair_send, pair_recv
        self.me = lax.axis_index("chan")
        self.chip, self.core = lax.div(self.me, 2), lax.rem(self.me, 2)
        self.spans = (pl.ds(0, cut), pl.ds(cut, x_ref.shape[0] - cut))
        self.ways = ({"chan": self.block(1)}, {"chan": self.block(-1)})
        self.twin = {"chan": self.chip * 2 + 1 - self.core}
        self.pairs = []

    def block(self, away):
        return lax.rem(self.chip + away + self.chips, self.chips) * 2 + self.core

    def refs(self, own, away, way, hop):
        source, landing = (self.x_ref if own else self.held.at[away]), self.held.at[away]
        if hop == self.hops:
            source, landing = source.at[self.spans[way]], landing.at[self.spans[way]]
        return source, landing

    def ring(self, way, hop):
        away = self.block(1 - hop if way == 0 else hop - 1)
        source, landing = self.refs(hop == 1, away, way, hop)
        send, recv, _, _ = self.sems
        return remote(source, landing, send.at[way, hop], recv.at[way, hop], self.ways[way])

    def pair(self, way, hop):
        away = self.block(-hop if way == 0 else hop)
        source, landing = self.refs(hop == 0, away, way, hop)
        _, _, send, recv = self.sems
        return remote(source, landing, send.at[way, hop], recv.at[way, hop], self.twin)

    def start(self):
        for way in range(2):
            self.ring(way, 1).start()
        self.pair(0, 0).start()
        self.pairs.append((0, 0))

    def advance(self, hop):
        for way in range(2):
            self.ring(way, hop).wait_recv()
            if hop < self.hops:
                self.ring(way, hop + 1).start()
            self.pair(way, hop).start()
            self.pairs.append((way, hop))

    def finish(self):
        for hop in range(1, self.hops + 1):
            for way in range(2):
                self.ring(way, hop).wait_send()
        for way, hop in self.pairs:
            self.pair(way, hop).wait()


def sum_kernel(rows, dps, chips, x_ref, y_ref, out_ref, all_ref, *scratch):
    main = Levels(rows, dps, x_ref, *scratch[:5], *scratch[10:12])
    side = Levels(rows, dps, y_ref, *scratch[5:10], *scratch[12:14])
    gathered = scratch[14]
    ring = Ring(chips, dps // 2, side.held, gathered, *scratch[15:])
    greet(main.places() + [*ring.ways, ring.twin])
    side.start(0)
    main.start(0)
    for level in range(3):
        side.arrive(level)
        main.arrive(level)
    side.arrive(3)
    ring.start()
    for hop in range(1, ring.hops + 1):
        ring.advance(hop)
    main.arrive(3)
    out_ref[...] = main.held[...]
    main.finish()
    side.finish()
    ring.finish()
    all_ref[...] = gathered[...]
    all_ref[ring.me] = side.held[...]


def group_sum(value, slices, collective_id):
    dps, rows = value.shape[:2]
    shares = lax.axis_size("chan")
    chips = shares // 2
    dtype = value.dtype
    buffers = []
    for shape in (value.shape, slices.shape):
        kinds = (shape, shape[1:], shape[1:], shape[2:], shape)
        buffers += [pltpu.VMEM(kind, dtype) for kind in kinds]
    gathered = (shares,) + slices.shape
    vmem = pl.BlockSpec(memory_space=pltpu.VMEM)
    return pl.pallas_call(
        functools.partial(sum_kernel, rows, dps, chips),
        out_shape=[
            jax.ShapeDtypeStruct(value.shape, dtype), jax.ShapeDtypeStruct(gathered, dtype)
        ],
        in_specs=[vmem] * 2,
        out_specs=[vmem] * 2,
        scratch_shapes=buffers
        + [pltpu.SemaphoreType.DMA((4, max(rows, dps)))] * 4
        + [pltpu.VMEM(gathered, dtype)]
        + [pltpu.SemaphoreType.DMA((2, chips // 2 + 1))] * 4,
        compiler_params=pltpu.CompilerParams(collective_id=collective_id, has_side_effects=True),
        cost_estimate=pl.CostEstimate(flops=0, bytes_accessed=100_000_000, transcendentals=0),
    )(value, slices)


def ring_kernel(chips, cut, deal, *refs):
    if not deal:
        x_ref, out_ref, held = refs[:3]
        ring = Ring(chips, cut, x_ref, held, *refs[3:])
        greet([*ring.ways, ring.twin])
        ring.start()
        for hop in range(1, ring.hops + 1):
            ring.advance(hop)
        ring.finish()
        out_ref[...] = held[...]
        out_ref[ring.me] = x_ref[...]
        return
    x_ref, y_ref, first_ref, last_ref, dealt_ref, held, dealt = refs[:7]
    deal_send, deal_recv, twin_send, twin_recv = refs[7:11]
    ring = Ring(chips, cut, x_ref, held, *refs[11:])
    greet([ring.twin] + [{"chan": ring.block(step)} for step in range(1, chips)])

    def direct(step):
        return remote(
            y_ref.at[lax.rem(ring.chip + step, chips)],
            dealt.at[ring.me],
            deal_send.at[step],
            deal_recv.at[step],
            {"chan": ring.block(step)},
        )

    def onward(step):
        slot = ring.block(-step)
        source = y_ref.at[ring.chip] if step == 0 else dealt.at[slot]
        return remote(source, dealt.at[slot], twin_send.at[step], twin_recv.at[step], ring.twin)

    ring.start()
    for step in range(1, chips):
        direct(step).start()
    onward(0).start()
    for hop in range(1, ring.hops):
        ring.advance(hop)
    for step in range(1, chips):
        direct(step).wait_recv()
        onward(step).start()
    ring.advance(ring.hops)
    ring.finish()
    for step in range(1, chips):
        direct(step).wait_send()
    for step in range(chips):
        onward(step).wait()
    first_ref[...] = held[:, :deal]
    last_ref[...] = held[:, deal:]
    first_ref[ring.me] = x_ref[:deal]
    last_ref[ring.me] = x_ref[deal:]
    dealt_ref[...] = dealt[...]
    dealt_ref[ring.me] = y_ref[ring.chip]


def ring_gather(value, cut, collective_id, dealt=None, split=0):
    shares = lax.axis_size("chan")
    chips = shares // 2
    held = (shares,) + value.shape
    if dealt is None:
        operands, outs, buffers, sems = [value], [held], [held], []
    else:
        slices = (shares,) + dealt.shape[1:]
        operands, buffers = [value, dealt], [held, slices]
        outs = [(shares, split, held[2]), (shares, held[1] - split, held[2]), slices]
        sems = [pltpu.SemaphoreType.DMA((chips,))] * 4
    vmem = pl.BlockSpec(memory_space=pltpu.VMEM)
    return pl.pallas_call(
        functools.partial(ring_kernel, chips, cut, split),
        out_shape=[jax.ShapeDtypeStruct(shape, value.dtype) for shape in outs],
        in_specs=[vmem] * len(operands),
        out_specs=[vmem] * len(outs),
        scratch_shapes=[pltpu.VMEM(shape, value.dtype) for shape in buffers]
        + sems
        + [pltpu.SemaphoreType.DMA((2, chips // 2 + 1))] * 4,
        compiler_params=pltpu.CompilerParams(collective_id=collective_id, has_side_effects=True),
        cost_estimate=pl.CostEstimate(flops=0, bytes_accessed=80_000_000, transcendentals=0),
    )(*operands)


def exchange(value, axis):
    return lax.all_to_all(value, axis, split_axis=0, concat_axis=0, tiled=True)


def window(source, left, top, cols, rows):
    return source[left : left + cols, top : top + rows]


def on_device(features_in, depth_weights, point_weights, proj_weights, cotangent):
    samples, band_rows, band_cols, channels = features_in.shape
    bands, shares, dps = lax.axis_size("row"), lax.axis_size("chan"), lax.axis_size("dp")
    branches, _, width = point_weights.shape
    weight_scale = 1.0 / math.sqrt(samples * dps * band_rows * bands * band_cols)
    half = band_rows // ROW_CLASSES
    cols = band_cols // COL_CLASSES
    rows = half * bands
    row_step, col_step = BASE_DILATION // ROW_CLASSES, BASE_DILATION // COL_CLASSES

    classes = features_in.reshape(half, ROW_CLASSES, cols, COL_CLASSES, channels)
    classes = classes.transpose(1, 3, 0, 2, 4).reshape(bands, half * cols, channels)
    cells = cotangent.reshape(half, ROW_CLASSES, COL_CLASSES, width).transpose(1, 2, 0, 3)
    cells = cells.reshape(bands, half, width)
    landed = exchange(
        jnp.concatenate([classes, cells[:, :, :channels], cells[:, :, channels:]], axis=1), "row"
    )
    area = half * cols
    grid = landed[:, :area].reshape(rows, cols, channels).transpose(1, 0, 2)
    cot = jnp.concatenate([landed[:, area : area + half], landed[:, area + half :]], axis=2)
    cot = cot.reshape(rows, width)
    full_point = ring_gather(
        point_weights.reshape(branches * channels, width), branches * channels // 2, 2
    )[0].reshape((shares,) + point_weights.shape)

    pads = ((3 * col_step, 3 * col_step), (3 * row_step, 3 * row_step), (0, 0))
    padded = jnp.pad(grid, pads)
    weights = depth_weights.astype(jnp.float32)
    maps = [grid]
    for level in range(1, branches):
        summed = jnp.zeros(grid.shape, jnp.float32)
        for i in range(3):
            for j in range(3):
                tap = window(
                    padded,
                    3 * col_step + (j - 1) * level * col_step,
                    3 * row_step + (i - 1) * level * row_step,
                    cols,
                    rows,
                )
                summed = summed + tap.astype(jnp.float32) * weights[level - 1, i, j]
        maps.append(summed.astype(jnp.bfloat16))
    spread, full_point = lax.optimization_barrier((jnp.stack(maps, axis=1), full_point))
    preact = jnp.einsum(
        "gbnk,gbkf->bnf",
        exchange(spread, "chan"),
        full_point,
        preferred_element_type=jnp.float32,
    )
    logistic = jax.nn.sigmoid(preact)
    activation = (preact * logistic).astype(jnp.bfloat16)
    act_grad = jnp.einsum("ng,bfg->bnf", cot, proj_weights, preferred_element_type=jnp.float32)
    pre_grad = (act_grad * logistic * (1.0 + preact * (1.0 - logistic))).astype(jnp.bfloat16)
    out_cells = jnp.einsum(
        "bnf,bfg->ng", activation, proj_weights, preferred_element_type=jnp.float32
    ).astype(jnp.bfloat16)

    chips = shares // 2
    per = chips // branches
    part, side = width // per, width // 2
    pieces = activation.reshape(branches, rows, per, part).transpose(0, 2, 1, 3)
    sent = jnp.concatenate([pre_grad.reshape(branches * rows, width), cot], axis=0)
    incoming, full_cot, slices = ring_gather(
        sent, sent.shape[0] // 32 * 16, 0, pieces.reshape(chips, rows, part), branches * rows
    )
    incoming = incoming.reshape(shares, branches, rows, width)
    core = lax.rem(lax.axis_index("chan"), 2)
    cot_side = lax.dynamic_slice_in_dim(full_cot, core * side, side, axis=2)
    proj_part = jnp.einsum(
        "xnf,xng->fg", slices, cot_side, preferred_element_type=jnp.float32
    )
    proj_part = jnp.concatenate([proj_part[: part // 2], proj_part[part // 2 :]], axis=1)
    group = bands * dps
    point_sum = jnp.einsum("xbnk,xbnf->bkf", spread, incoming, preferred_element_type=jnp.float32)
    spread_grad = jnp.einsum(
        "xbnf,bkf->bxnk", incoming, point_weights, preferred_element_type=jnp.float32
    ).astype(jnp.bfloat16)
    grad_in = spread_grad[0].astype(jnp.float32)
    depth_sums = []
    for level in range(1, branches):
        branch_grad = spread_grad[level].astype(jnp.float32)
        grad_padded = jnp.pad(spread_grad[level], pads)
        for i in range(3):
            for j in range(3):
                left, top = (j - 1) * level * col_step, (i - 1) * level * row_step
                tap = window(padded, 3 * col_step + left, 3 * row_step + top, cols, rows)
                depth_sums.append(jnp.sum(tap.astype(jnp.float32) * branch_grad, axis=(0, 1)))
                grad_tap = window(
                    grad_padded, 3 * col_step - left, 3 * row_step - top, cols, rows
                )
                grad_in = grad_in + grad_tap.astype(jnp.float32) * weights[level - 1, i, j]
    returned = grad_in.astype(jnp.bfloat16).transpose(1, 0, 2).reshape(bands, area, channels)
    out_cells = out_cells.reshape(bands, half, width)
    leaving = jnp.concatenate(
        [returned, out_cells[:, :, :channels], out_cells[:, :, channels:]], axis=1
    )
    taps = len(depth_sums)
    depth_part = jnp.pad(jnp.stack(depth_sums), ((0, group - taps), (0, width - channels)))
    height = branches * channels // group
    terms = jnp.concatenate(
        [point_sum.reshape(group, height, width), depth_part[:, None]], axis=1
    ).astype(jnp.bfloat16)
    leaving, terms = lax.optimization_barrier((leaving, terms))
    returned = exchange(leaving, "row")
    output = jnp.concatenate(
        [returned[:, area : area + half], returned[:, area + half :]], axis=2
    )
    output = output.reshape(ROW_CLASSES, COL_CLASSES, half, width).transpose(2, 0, 1, 3)
    output = output.reshape(1, band_rows, COL_CLASSES, width)
    grad_input = returned[:, :area].reshape(ROW_CLASSES, COL_CLASSES, half, cols, channels)
    grad_input = grad_input.transpose(2, 0, 3, 1, 4).reshape(features_in.shape)

    summed, grad_proj = group_sum(
        terms.reshape(dps, bands, height + 1, width),
        proj_part.astype(jnp.bfloat16).reshape(dps, bands, -1, width),
        1,
    )
    summed = summed.reshape(group, height + 1, width)
    grad_point = summed[:, :height].reshape(point_weights.shape).astype(jnp.float32) * weight_scale
    grad_depth = summed[:taps, height, :channels].reshape(depth_weights.shape)
    grad_depth = grad_depth.astype(jnp.float32) * weight_scale
    grad_proj = grad_proj.reshape(branches, per, 2, part // 2, 2, side).transpose(0, 1, 4, 3, 2, 5)
    grad_proj = grad_proj.reshape(branches, width, width).astype(jnp.float32) * weight_scale
    return (output, grad_input, grad_depth, grad_point, grad_proj)


def solution(mesh):
    in_specs = (
        P("dp", "row", None, "chan"),
        P(None, None, None, "chan"),
        P(None, "chan", None),
        P(),
        P("dp", "row", "chan", None),
    )
    out_specs = (
        P("dp", "row", "chan", None),
        P("dp", "row", None, "chan"),
        P(None, None, None, "chan"),
        P(None, "chan", None),
        P(),
    )
    return jax.shard_map(
        on_device, mesh=mesh, in_specs=in_specs, out_specs=out_specs, check_vma=False
    )
```

```python
import functools
import math

import jax
import jax.numpy as jnp
from jax import lax
from jax.experimental import pallas as pl
from jax.experimental.pallas import tpu as pltpu
from jax.sharding import PartitionSpec as P

BASE_DILATION = 12
ROW_CLASSES = 2
COL_CLASSES = 4
CHUNKS = 4
MESH = pl.DeviceIdType.MESH


def remote(source, landing, send_sem, recv_sem, where):
    return pltpu.make_async_remote_copy(
        src_ref=source,
        dst_ref=landing,
        send_sem=send_sem,
        recv_sem=recv_sem,
        device_id=where,
        device_id_type=MESH,
    )


def greet(places):
    barrier = pltpu.get_barrier_semaphore()
    for where in places:
        pl.semaphore_signal(barrier, inc=1, device_id=where, device_id_type=MESH)
    pl.semaphore_wait(barrier, len(places))


class Levels:
    def __init__(self, rows, dps, x_ref, land1, part, land2, total, held, send, recv):
        self.rows, self.dps, self.x_ref = rows, dps, x_ref
        self.land1, self.part, self.land2, self.total, self.held = land1, part, land2, total, held
        self.send, self.recv = send, recv
        self.row, self.dp = lax.axis_index("row"), lax.axis_index("dp")

    def dp_peer(self, step):
        return lax.rem(self.dp + step, self.dps)

    def row_peer(self, step):
        return lax.rem(self.row + step, self.rows)

    def places(self):
        found = [{"dp": self.dp_peer(step)} for step in range(1, self.dps)]
        return found + [{"row": self.row_peer(step)} for step in range(1, self.rows)]

    def steps(self, level):
        return range(1, self.dps if level in (0, 3) else self.rows)

    def copy(self, level, step):
        if level in (0, 3):
            peer, where = self.dp_peer(step), {"dp": self.dp_peer(step)}
        else:
            peer, where = self.row_peer(step), {"row": self.row_peer(step)}
        source, landing = (
            lambda: (self.x_ref.at[peer], self.land1.at[step]),
            lambda: (self.part.at[peer], self.land2.at[step]),
            lambda: (self.total, self.held.at[self.dp, self.row]),
            lambda: (self.held.at[self.dp], self.held.at[self.dp]),
        )[level]()
        return remote(source, landing, self.send.at[level, step], self.recv.at[level, step], where)

    def start(self, level):
        for step in self.steps(level):
            self.copy(level, step).start()

    def arrive(self, level):
        if level == 0:
            summed = self.x_ref[self.dp].astype(jnp.float32)
        elif level == 1:
            summed = self.part[self.row].astype(jnp.float32)
        for step in self.steps(level):
            self.copy(level, step).wait_recv()
            if level == 0:
                summed = summed + self.land1[step].astype(jnp.float32)
            elif level == 1:
                summed = summed + self.land2[step].astype(jnp.float32)
        if level == 0:
            self.part[...] = summed.astype(self.part.dtype)
        elif level == 1:
            self.total[...] = summed.astype(self.total.dtype)
            self.held[self.dp, self.row] = self.total[...]
        if level < 3:
            self.start(level + 1)

    def finish(self):
        for level in range(4):
            for step in self.steps(level):
                self.copy(level, step).wait_send()


class Ring:
    def __init__(self, chips, chunk, x_ref, held, ring_send, ring_recv, pair_send, pair_recv):
        self.chips, self.hops, self.x_ref, self.held = chips, chips // 2, x_ref, held
        self.sems = ring_send, ring_recv, pair_send, pair_recv
        self.me = lax.axis_index("chan")
        self.chip, self.core = lax.div(self.me, 2), lax.rem(self.me, 2)
        size = x_ref.shape[0]
        self.spans = [pl.ds(at, min(chunk, size - at)) for at in range(0, size, chunk)]
        self.ways = ({"chan": self.block(1)}, {"chan": self.block(-1)})
        self.twin = {"chan": self.chip * 2 + 1 - self.core}
        self.pairs = []

    def block(self, away):
        return lax.rem(self.chip + away + self.chips, self.chips) * 2 + self.core

    def brings(self, way, hop, chunk):
        return hop < self.hops or (chunk < len(self.spans) // 2) == (way == 0)

    def refs(self, own, away, chunk):
        landing = self.held.at[away].at[self.spans[chunk]]
        return (self.x_ref.at[self.spans[chunk]] if own else landing), landing

    def ring(self, way, hop, chunk):
        source, landing = self.refs(hop == 1, self.block(1 - hop if way == 0 else hop - 1), chunk)
        at = (way, hop, chunk)
        send, recv, _, _ = self.sems
        return remote(source, landing, send.at[at], recv.at[at], self.ways[way])

    def pair(self, way, hop, chunk):
        source, landing = self.refs(hop == 0, self.block(-hop if way == 0 else hop), chunk)
        at = (way, hop, chunk)
        _, _, send, recv = self.sems
        return remote(source, landing, send.at[at], recv.at[at], self.twin)

    def both(self, way, hop, chunk):
        self.pair(way, hop, chunk).start()
        self.pairs.append((way, hop, chunk))

    def start(self):
        for chunk in range(len(self.spans)):
            for way in range(2):
                self.ring(way, 1, chunk).start()
        for chunk in range(len(self.spans)):
            self.both(0, 0, chunk)

    def advance(self, hop):
        for chunk in range(len(self.spans)):
            for way in range(2):
                if self.brings(way, hop, chunk):
                    self.ring(way, hop, chunk).wait_recv()
                    if hop < self.hops and self.brings(way, hop + 1, chunk):
                        self.ring(way, hop + 1, chunk).start()
                    self.both(way, hop, chunk)

    def finish(self):
        for way, hop, chunk in self.pairs:
            if hop:
                self.ring(way, hop, chunk).wait_send()
            self.pair(way, hop, chunk).wait()


def sum_kernel(rows, dps, chips, x_ref, y_ref, out_ref, all_ref, *scratch):
    main = Levels(rows, dps, x_ref, *scratch[:5], *scratch[10:12])
    side = Levels(rows, dps, y_ref, *scratch[5:10], *scratch[12:14])
    gathered = scratch[14]
    ring = Ring(chips, dps // 2, side.held, gathered, *scratch[15:])
    greet(main.places() + [*ring.ways, ring.twin])
    side.start(0)
    main.start(0)
    side.arrive(0)
    side.arrive(1)
    main.arrive(0)
    side.arrive(2)
    side.arrive(3)
    ring.start()
    main.arrive(1)
    for hop in range(1, ring.hops):
        ring.advance(hop)
    main.arrive(2)
    ring.advance(ring.hops)
    main.arrive(3)
    out_ref[...] = main.held[...]
    main.finish()
    side.finish()
    ring.finish()
    all_ref[...] = gathered[...]
    all_ref[ring.me] = side.held[...]


def group_sum(value, slices, collective_id):
    dps, rows = value.shape[:2]
    shares = lax.axis_size("chan")
    chips = shares // 2
    dtype = value.dtype
    buffers = []
    for shape in (value.shape, slices.shape):
        kinds = (shape, shape[1:], shape[1:], shape[2:], shape)
        buffers += [pltpu.VMEM(kind, dtype) for kind in kinds]
    gathered = (shares,) + slices.shape
    vmem = pl.BlockSpec(memory_space=pltpu.VMEM)
    return pl.pallas_call(
        functools.partial(sum_kernel, rows, dps, chips),
        out_shape=[
            jax.ShapeDtypeStruct(value.shape, dtype), jax.ShapeDtypeStruct(gathered, dtype)
        ],
        in_specs=[vmem] * 2,
        out_specs=[vmem] * 2,
        scratch_shapes=buffers
        + [pltpu.SemaphoreType.DMA((4, max(rows, dps)))] * 4
        + [pltpu.VMEM(gathered, dtype)]
        + [pltpu.SemaphoreType.DMA((2, chips // 2 + 1, 2))] * 4,
        compiler_params=pltpu.CompilerParams(collective_id=collective_id, has_side_effects=True),
        cost_estimate=pl.CostEstimate(flops=0, bytes_accessed=100_000_000, transcendentals=0),
    )(value, slices)


def ring_kernel(chips, chunk, deal, *refs):
    if not deal:
        x_ref, out_ref, held = refs[:3]
        ring = Ring(chips, chunk, x_ref, held, *refs[3:])
        greet([*ring.ways, ring.twin])
        ring.start()
        for hop in range(1, ring.hops + 1):
            ring.advance(hop)
        ring.finish()
        out_ref[...] = held[...]
        out_ref[ring.me] = x_ref[...]
        return
    x_ref, y_ref, first_ref, last_ref, dealt_ref, held, dealt = refs[:7]
    deal_send, deal_recv, twin_send, twin_recv = refs[7:11]
    ring = Ring(chips, chunk, x_ref, held, *refs[11:])
    greet([ring.twin] + [{"chan": ring.block(step)} for step in range(1, chips)])

    def direct(step):
        return remote(
            y_ref.at[lax.rem(ring.chip + step, chips)],
            dealt.at[ring.me],
            deal_send.at[step],
            deal_recv.at[step],
            {"chan": ring.block(step)},
        )

    def onward(step):
        slot = ring.block(-step)
        source = y_ref.at[ring.chip] if step == 0 else dealt.at[slot]
        return remote(source, dealt.at[slot], twin_send.at[step], twin_recv.at[step], ring.twin)

    ring.start()
    for step in range(1, chips):
        direct(step).start()
    onward(0).start()
    for hop in range(1, ring.hops):
        ring.advance(hop)
    for step in range(1, chips):
        direct(step).wait_recv()
        onward(step).start()
    ring.advance(ring.hops)
    ring.finish()
    for step in range(1, chips):
        direct(step).wait_send()
    for step in range(chips):
        onward(step).wait()
    first_ref[...] = held[:, :deal]
    last_ref[...] = held[:, deal:]
    first_ref[ring.me] = x_ref[:deal]
    last_ref[ring.me] = x_ref[deal:]
    dealt_ref[...] = dealt[...]
    dealt_ref[ring.me] = y_ref[ring.chip]


def ring_gather(value, chunk, collective_id, dealt=None, split=0):
    shares = lax.axis_size("chan")
    chips = shares // 2
    held = (shares,) + value.shape
    if dealt is None:
        operands, outs, buffers, sems = [value], [held], [held], []
    else:
        slices = (shares,) + dealt.shape[1:]
        operands, buffers = [value, dealt], [held, slices]
        outs = [(shares, split, held[2]), (shares, held[1] - split, held[2]), slices]
        sems = [pltpu.SemaphoreType.DMA((chips,))] * 4
    vmem = pl.BlockSpec(memory_space=pltpu.VMEM)
    return pl.pallas_call(
        functools.partial(ring_kernel, chips, chunk, split),
        out_shape=[jax.ShapeDtypeStruct(shape, value.dtype) for shape in outs],
        in_specs=[vmem] * len(operands),
        out_specs=[vmem] * len(outs),
        scratch_shapes=[pltpu.VMEM(shape, value.dtype) for shape in buffers]
        + sems
        + [pltpu.SemaphoreType.DMA((2, chips // 2 + 1, -(-value.shape[0] // chunk)))] * 4,
        compiler_params=pltpu.CompilerParams(collective_id=collective_id, has_side_effects=True),
        cost_estimate=pl.CostEstimate(flops=0, bytes_accessed=80_000_000, transcendentals=0),
    )(*operands)


def exchange(value, axis):
    return lax.all_to_all(value, axis, split_axis=0, concat_axis=0, tiled=True)


def window(source, left, top, cols, rows):
    return source[left : left + cols, top : top + rows]


def on_device(features_in, depth_weights, point_weights, proj_weights, cotangent):
    samples, band_rows, band_cols, channels = features_in.shape
    bands, shares, dps = lax.axis_size("row"), lax.axis_size("chan"), lax.axis_size("dp")
    branches, _, width = point_weights.shape
    weight_scale = 1.0 / math.sqrt(samples * dps * band_rows * bands * band_cols)
    half = band_rows // ROW_CLASSES
    cols = band_cols // COL_CLASSES
    rows = half * bands
    row_step, col_step = BASE_DILATION // ROW_CLASSES, BASE_DILATION // COL_CLASSES

    classes = features_in.reshape(half, ROW_CLASSES, cols, COL_CLASSES, channels)
    classes = classes.transpose(1, 3, 0, 2, 4).reshape(bands, half * cols, channels)
    cells = cotangent.reshape(half, ROW_CLASSES, COL_CLASSES, width).transpose(1, 2, 0, 3)
    cells = cells.reshape(bands, half, width)
    landed = exchange(
        jnp.concatenate([classes, cells[:, :, :channels], cells[:, :, channels:]], axis=1), "row"
    )
    area = half * cols
    grid = landed[:, :area].reshape(rows, cols, channels).transpose(1, 0, 2)
    cot = jnp.concatenate([landed[:, area : area + half], landed[:, area + half :]], axis=2)
    cot = cot.reshape(rows, width)
    full_point = ring_gather(
        point_weights.reshape(branches * channels, width), branches * channels // CHUNKS, 2
    )[0].reshape((shares,) + point_weights.shape)

    pads = ((3 * col_step, 3 * col_step), (3 * row_step, 3 * row_step), (0, 0))
    padded = jnp.pad(grid, pads)
    weights = depth_weights.astype(jnp.float32)
    maps = [grid]
    for level in range(1, branches):
        summed = jnp.zeros(grid.shape, jnp.float32)
        for i in range(3):
            for j in range(3):
                tap = window(
                    padded,
                    3 * col_step + (j - 1) * level * col_step,
                    3 * row_step + (i - 1) * level * row_step,
                    cols,
                    rows,
                )
                summed = summed + tap.astype(jnp.float32) * weights[level - 1, i, j]
        maps.append(summed.astype(jnp.bfloat16))
    spread, full_point = lax.optimization_barrier((jnp.stack(maps, axis=1), full_point))
    preact = jnp.einsum(
        "gbnk,gbkf->bnf",
        exchange(spread, "chan"),
        full_point,
        preferred_element_type=jnp.float32,
    )
    logistic = jax.nn.sigmoid(preact)
    activation = (preact * logistic).astype(jnp.bfloat16)
    act_grad = jnp.einsum("ng,bfg->bnf", cot, proj_weights, preferred_element_type=jnp.float32)
    pre_grad = (act_grad * logistic * (1.0 + preact * (1.0 - logistic))).astype(jnp.bfloat16)
    out_cells = jnp.einsum(
        "bnf,bfg->ng", activation, proj_weights, preferred_element_type=jnp.float32
    ).astype(jnp.bfloat16)

    chips = shares // 2
    per = chips // branches
    part, side = width // per, width // 2
    pieces = activation.reshape(branches, rows, per, part).transpose(0, 2, 1, 3)
    sent = jnp.concatenate([pre_grad.reshape(branches * rows, width), cot], axis=0)
    incoming, full_cot, slices = ring_gather(
        sent, -(-sent.shape[0] // CHUNKS // 16) * 16, 0, pieces.reshape(chips, rows, part), branches * rows
    )
    incoming = incoming.reshape(shares, branches, rows, width)
    core = lax.rem(lax.axis_index("chan"), 2)
    cot_side = lax.dynamic_slice_in_dim(full_cot, core * side, side, axis=2)
    proj_part = jnp.einsum(
        "xnf,xng->fg", slices, cot_side, preferred_element_type=jnp.float32
    )
    proj_part = jnp.concatenate([proj_part[: part // 2], proj_part[part // 2 :]], axis=1)
    group = bands * dps
    point_sum = jnp.einsum("xbnk,xbnf->bkf", spread, incoming, preferred_element_type=jnp.float32)
    spread_grad = jnp.einsum(
        "xbnf,bkf->bxnk", incoming, point_weights, preferred_element_type=jnp.float32
    ).astype(jnp.bfloat16)
    grad_in = spread_grad[0].astype(jnp.float32)
    depth_sums = []
    for level in range(1, branches):
        branch_grad = spread_grad[level].astype(jnp.float32)
        grad_padded = jnp.pad(spread_grad[level], pads)
        for i in range(3):
            for j in range(3):
                left, top = (j - 1) * level * col_step, (i - 1) * level * row_step
                tap = window(padded, 3 * col_step + left, 3 * row_step + top, cols, rows)
                depth_sums.append(jnp.sum(tap.astype(jnp.float32) * branch_grad, axis=(0, 1)))
                grad_tap = window(
                    grad_padded, 3 * col_step - left, 3 * row_step - top, cols, rows
                )
                grad_in = grad_in + grad_tap.astype(jnp.float32) * weights[level - 1, i, j]
    returned = grad_in.astype(jnp.bfloat16).transpose(1, 0, 2).reshape(bands, area, channels)
    out_cells = out_cells.reshape(bands, half, width)
    leaving = jnp.concatenate(
        [returned, out_cells[:, :, :channels], out_cells[:, :, channels:]], axis=1
    )
    taps = len(depth_sums)
    depth_part = jnp.pad(jnp.stack(depth_sums), ((0, group - taps), (0, width - channels)))
    height = branches * channels // group
    terms = jnp.concatenate(
        [point_sum.reshape(group, height, width), depth_part[:, None]], axis=1
    ).astype(jnp.bfloat16)
    leaving, terms = lax.optimization_barrier((leaving, terms))
    returned = exchange(leaving, "row")
    output = jnp.concatenate(
        [returned[:, area : area + half], returned[:, area + half :]], axis=2
    )
    output = output.reshape(ROW_CLASSES, COL_CLASSES, half, width).transpose(2, 0, 1, 3)
    output = output.reshape(1, band_rows, COL_CLASSES, width)
    grad_input = returned[:, :area].reshape(ROW_CLASSES, COL_CLASSES, half, cols, channels)
    grad_input = grad_input.transpose(2, 0, 3, 1, 4).reshape(features_in.shape)

    summed, grad_proj = group_sum(
        terms.reshape(dps, bands, height + 1, width),
        proj_part.astype(jnp.bfloat16).reshape(dps, bands, -1, width),
        1,
    )
    summed = summed.reshape(group, height + 1, width)
    grad_point = summed[:, :height].reshape(point_weights.shape).astype(jnp.float32) * weight_scale
    grad_depth = summed[:taps, height, :channels].reshape(depth_weights.shape)
    grad_depth = grad_depth.astype(jnp.float32) * weight_scale
    grad_proj = grad_proj.reshape(branches, per, 2, part // 2, 2, side).transpose(0, 1, 4, 3, 2, 5)
    grad_proj = grad_proj.reshape(branches, width, width).astype(jnp.float32) * weight_scale
    return (output, grad_input, grad_depth, grad_point, grad_proj)


def solution(mesh):
    in_specs = (
        P("dp", "row", None, "chan"),
        P(None, None, None, "chan"),
        P(None, "chan", None),
        P(),
        P("dp", "row", "chan", None),
    )
    out_specs = (
        P("dp", "row", "chan", None),
        P("dp", "row", None, "chan"),
        P(None, None, None, "chan"),
        P(None, "chan", None),
        P(),
    )
    return jax.shard_map(
        on_device, mesh=mesh, in_specs=in_specs, out_specs=out_specs, check_vma=False
    )
```

```python
import functools
import math

import jax
import jax.numpy as jnp
from jax import lax
from jax.experimental import pallas as pl
from jax.experimental.pallas import tpu as pltpu
from jax.sharding import PartitionSpec as P

BASE_DILATION = 12
ROW_CLASSES = 2
COL_CLASSES = 4
CHUNKS = 4
MESH = pl.DeviceIdType.MESH


def remote(source, landing, send_sem, recv_sem, where):
    return pltpu.make_async_remote_copy(
        src_ref=source,
        dst_ref=landing,
        send_sem=send_sem,
        recv_sem=recv_sem,
        device_id=where,
        device_id_type=MESH,
    )


def greet(places):
    barrier = pltpu.get_barrier_semaphore()
    for where in places:
        pl.semaphore_signal(barrier, inc=1, device_id=where, device_id_type=MESH)
    pl.semaphore_wait(barrier, len(places))


class Levels:
    def __init__(self, rows, dps, x_ref, land1, part, land2, total, held, send, recv):
        self.rows, self.dps, self.x_ref = rows, dps, x_ref
        self.land1, self.part, self.land2, self.total, self.held = land1, part, land2, total, held
        self.send, self.recv = send, recv
        self.row, self.dp = lax.axis_index("row"), lax.axis_index("dp")

    def dp_peer(self, step):
        return lax.rem(self.dp + step, self.dps)

    def row_peer(self, step):
        return lax.rem(self.row + step, self.rows)

    def places(self):
        found = [{"dp": self.dp_peer(step)} for step in range(1, self.dps)]
        return found + [{"row": self.row_peer(step)} for step in range(1, self.rows)]

    def steps(self, level):
        return range(1, self.dps if level in (0, 3) else self.rows)

    def copy(self, level, step):
        if level in (0, 3):
            peer, where = self.dp_peer(step), {"dp": self.dp_peer(step)}
        else:
            peer, where = self.row_peer(step), {"row": self.row_peer(step)}
        source, landing = (
            lambda: (self.x_ref.at[peer], self.land1.at[step]),
            lambda: (self.part.at[peer], self.land2.at[step]),
            lambda: (self.total, self.held.at[self.dp, self.row]),
            lambda: (self.held.at[self.dp], self.held.at[self.dp]),
        )[level]()
        return remote(source, landing, self.send.at[level, step], self.recv.at[level, step], where)

    def start(self, level):
        for step in self.steps(level):
            self.copy(level, step).start()

    def arrive(self, level):
        if level == 0:
            summed = self.x_ref[self.dp].astype(jnp.float32)
        elif level == 1:
            summed = self.part[self.row].astype(jnp.float32)
        for step in self.steps(level):
            self.copy(level, step).wait_recv()
            if level == 0:
                summed = summed + self.land1[step].astype(jnp.float32)
            elif level == 1:
                summed = summed + self.land2[step].astype(jnp.float32)
        if level == 0:
            self.part[...] = summed.astype(self.part.dtype)
        elif level == 1:
            self.total[...] = summed.astype(self.total.dtype)
            self.held[self.dp, self.row] = self.total[...]
        if level < 3:
            self.start(level + 1)

    def finish(self):
        for level in range(4):
            for step in self.steps(level):
                self.copy(level, step).wait_send()


class Ring:
    def __init__(self, chips, chunk, x_ref, held, ring_send, ring_recv, pair_send, pair_recv):
        self.chips, self.hops, self.x_ref, self.held = chips, chips // 2, x_ref, held
        self.sems = ring_send, ring_recv, pair_send, pair_recv
        self.me = lax.axis_index("chan")
        self.chip, self.core = lax.div(self.me, 2), lax.rem(self.me, 2)
        size = x_ref.shape[0]
        self.spans = [pl.ds(at, min(chunk, size - at)) for at in range(0, size, chunk)]
        self.ways = ({"chan": self.block(1)}, {"chan": self.block(-1)})
        self.twin = {"chan": self.chip * 2 + 1 - self.core}
        self.pairs = []

    def block(self, away):
        return lax.rem(self.chip + away + self.chips, self.chips) * 2 + self.core

    def brings(self, way, hop, chunk):
        return hop < self.hops or (chunk < len(self.spans) // 2) == (way == 0)

    def refs(self, own, away, chunk):
        landing = self.held.at[away].at[self.spans[chunk]]
        return (self.x_ref.at[self.spans[chunk]] if own else landing), landing

    def ring(self, way, hop, chunk):
        source, landing = self.refs(hop == 1, self.block(1 - hop if way == 0 else hop - 1), chunk)
        at = (way, hop, chunk)
        send, recv, _, _ = self.sems
        return remote(source, landing, send.at[at], recv.at[at], self.ways[way])

    def pair(self, way, hop, chunk):
        source, landing = self.refs(hop == 0, self.block(-hop if way == 0 else hop), chunk)
        at = (way, hop, chunk)
        _, _, send, recv = self.sems
        return remote(source, landing, send.at[at], recv.at[at], self.twin)

    def both(self, way, hop, chunk):
        self.pair(way, hop, chunk).start()
        self.pairs.append((way, hop, chunk))

    def start(self):
        for chunk in range(len(self.spans)):
            for way in range(2):
                self.ring(way, 1, chunk).start()
        for chunk in range(len(self.spans)):
            self.both(0, 0, chunk)

    def advance(self, hop):
        for chunk in range(len(self.spans)):
            for way in range(2):
                if self.brings(way, hop, chunk):
                    self.ring(way, hop, chunk).wait_recv()
                    if hop < self.hops and self.brings(way, hop + 1, chunk):
                        self.ring(way, hop + 1, chunk).start()
                    self.both(way, hop, chunk)

    def finish(self):
        for way, hop, chunk in self.pairs:
            if hop:
                self.ring(way, hop, chunk).wait_send()
            self.pair(way, hop, chunk).wait()


def sum_kernel(rows, dps, chips, take, x_ref, y_ref, out_ref, side_ref, all_ref, *scratch):
    main = Levels(rows, dps, x_ref, *scratch[:5], *scratch[10:12])
    side = Levels(rows, dps, y_ref, *scratch[5:10], *scratch[12:14])
    gathered, packed = scratch[14:16]
    ring = Ring(chips, packed.shape[0] // 2, packed, gathered, *scratch[16:])
    greet(main.places() + [*ring.ways, ring.twin])
    side.start(0)
    main.start(0)
    side.arrive(0)
    side.arrive(1)
    main.arrive(0)
    side.arrive(2)
    side.arrive(3)
    for dp in range(dps):
        for row in range(rows):
            at = (dp * rows + row) * take
            packed[at : at + take] = side.held[dp, row, :take]
    ring.start()
    main.arrive(1)
    for hop in range(1, ring.hops):
        ring.advance(hop)
    main.arrive(2)
    ring.advance(ring.hops)
    main.arrive(3)
    out_ref[...] = main.held[...]
    main.finish()
    side.finish()
    ring.finish()
    side_ref[...] = side.held[...]
    all_ref[...] = gathered[...]
    all_ref[ring.me] = packed[...]


def group_sum(value, slices, take, collective_id):
    dps, rows = value.shape[:2]
    shares = lax.axis_size("chan")
    chips = shares // 2
    dtype = value.dtype
    buffers = []
    for shape in (value.shape, slices.shape):
        kinds = (shape, shape[1:], shape[1:], shape[2:], shape)
        buffers += [pltpu.VMEM(kind, dtype) for kind in kinds]
    packed = (dps * rows * take, slices.shape[3])
    gathered = (shares,) + packed
    vmem = pl.BlockSpec(memory_space=pltpu.VMEM)
    return pl.pallas_call(
        functools.partial(sum_kernel, rows, dps, chips, take),
        out_shape=[
            jax.ShapeDtypeStruct(shape, dtype) for shape in (value.shape, slices.shape, gathered)
        ],
        in_specs=[vmem] * 2,
        out_specs=[vmem] * 3,
        scratch_shapes=buffers
        + [pltpu.SemaphoreType.DMA((4, max(rows, dps)))] * 4
        + [pltpu.VMEM(gathered, dtype), pltpu.VMEM(packed, dtype)]
        + [pltpu.SemaphoreType.DMA((2, chips // 2 + 1, 2))] * 4,
        compiler_params=pltpu.CompilerParams(collective_id=collective_id, has_side_effects=True),
        cost_estimate=pl.CostEstimate(flops=0, bytes_accessed=100_000_000, transcendentals=0),
    )(value, slices)


def ring_kernel(chips, chunk, deal, *refs):
    if not deal:
        x_ref, out_ref, held = refs[:3]
        ring = Ring(chips, chunk, x_ref, held, *refs[3:])
        greet([*ring.ways, ring.twin])
        ring.start()
        for hop in range(1, ring.hops + 1):
            ring.advance(hop)
        ring.finish()
        out_ref[...] = held[...]
        out_ref[ring.me] = x_ref[...]
        return
    x_ref, y_ref, first_ref, last_ref, dealt_ref, held, dealt = refs[:7]
    deal_send, deal_recv, twin_send, twin_recv = refs[7:11]
    ring = Ring(chips, chunk, x_ref, held, *refs[11:])
    greet([ring.twin] + [{"chan": ring.block(step)} for step in range(1, chips)])

    def direct(step):
        return remote(
            y_ref.at[lax.rem(ring.chip + step, chips)],
            dealt.at[ring.me],
            deal_send.at[step],
            deal_recv.at[step],
            {"chan": ring.block(step)},
        )

    def onward(step):
        slot = ring.block(-step)
        source = y_ref.at[ring.chip] if step == 0 else dealt.at[slot]
        return remote(source, dealt.at[slot], twin_send.at[step], twin_recv.at[step], ring.twin)

    ring.start()
    for step in range(1, chips):
        direct(step).start()
    onward(0).start()
    for hop in range(1, ring.hops):
        ring.advance(hop)
    for step in range(1, chips):
        direct(step).wait_recv()
        onward(step).start()
    ring.advance(ring.hops)
    ring.finish()
    for step in range(1, chips):
        direct(step).wait_send()
    for step in range(chips):
        onward(step).wait()
    first_ref[...] = held[:, :deal]
    last_ref[...] = held[:, deal:]
    first_ref[ring.me] = x_ref[:deal]
    last_ref[ring.me] = x_ref[deal:]
    dealt_ref[...] = dealt[...]
    dealt_ref[ring.me] = y_ref[ring.chip]


def ring_gather(value, chunk, collective_id, dealt=None, split=0):
    shares = lax.axis_size("chan")
    chips = shares // 2
    held = (shares,) + value.shape
    if dealt is None:
        operands, outs, buffers, sems = [value], [held], [held], []
    else:
        slices = (shares,) + dealt.shape[1:]
        operands, buffers = [value, dealt], [held, slices]
        outs = [(shares, split, held[2]), (shares, held[1] - split, held[2]), slices]
        sems = [pltpu.SemaphoreType.DMA((chips,))] * 4
    vmem = pl.BlockSpec(memory_space=pltpu.VMEM)
    return pl.pallas_call(
        functools.partial(ring_kernel, chips, chunk, split),
        out_shape=[jax.ShapeDtypeStruct(shape, value.dtype) for shape in outs],
        in_specs=[vmem] * len(operands),
        out_specs=[vmem] * len(outs),
        scratch_shapes=[pltpu.VMEM(shape, value.dtype) for shape in buffers]
        + sems
        + [pltpu.SemaphoreType.DMA((2, chips // 2 + 1, -(-value.shape[0] // chunk)))] * 4,
        compiler_params=pltpu.CompilerParams(collective_id=collective_id, has_side_effects=True),
        cost_estimate=pl.CostEstimate(flops=0, bytes_accessed=80_000_000, transcendentals=0),
    )(*operands)


def exchange(value, axis):
    return lax.all_to_all(value, axis, split_axis=0, concat_axis=0, tiled=True)


def window(source, left, top, cols, rows):
    return source[left : left + cols, top : top + rows]


def on_device(features_in, depth_weights, point_weights, proj_weights, cotangent):
    samples, band_rows, band_cols, channels = features_in.shape
    bands, shares, dps = lax.axis_size("row"), lax.axis_size("chan"), lax.axis_size("dp")
    branches, _, width = point_weights.shape
    weight_scale = 1.0 / math.sqrt(samples * dps * band_rows * bands * band_cols)
    half = band_rows // ROW_CLASSES
    cols = band_cols // COL_CLASSES
    rows = half * bands
    row_step, col_step = BASE_DILATION // ROW_CLASSES, BASE_DILATION // COL_CLASSES

    classes = features_in.reshape(half, ROW_CLASSES, cols, COL_CLASSES, channels)
    classes = classes.transpose(1, 3, 0, 2, 4).reshape(bands, half * cols, channels)
    cells = cotangent.reshape(half, ROW_CLASSES, COL_CLASSES, width).transpose(1, 2, 0, 3)
    cells = cells.reshape(bands, half, width)
    landed = exchange(
        jnp.concatenate([classes, cells[:, :, :channels], cells[:, :, channels:]], axis=1), "row"
    )
    area = half * cols
    grid = landed[:, :area].reshape(rows, cols, channels).transpose(1, 0, 2)
    cot = jnp.concatenate([landed[:, area : area + half], landed[:, area + half :]], axis=2)
    cot = cot.reshape(rows, width)
    full_point = ring_gather(
        point_weights.reshape(branches * channels, width), branches * channels // CHUNKS, 2
    )[0].reshape((shares,) + point_weights.shape)

    pads = ((3 * col_step, 3 * col_step), (3 * row_step, 3 * row_step), (0, 0))
    padded = jnp.pad(grid, pads)
    weights = depth_weights.astype(jnp.float32)
    maps = [grid]
    for level in range(1, branches):
        summed = jnp.zeros(grid.shape, jnp.float32)
        for i in range(3):
            for j in range(3):
                tap = window(
                    padded,
                    3 * col_step + (j - 1) * level * col_step,
                    3 * row_step + (i - 1) * level * row_step,
                    cols,
                    rows,
                )
                summed = summed + tap.astype(jnp.float32) * weights[level - 1, i, j]
        maps.append(summed.astype(jnp.bfloat16))
    spread, full_point = lax.optimization_barrier((jnp.stack(maps, axis=1), full_point))
    preact = jnp.einsum(
        "gbnk,gbkf->bnf",
        exchange(spread, "chan"),
        full_point,
        preferred_element_type=jnp.float32,
    )
    logistic = jax.nn.sigmoid(preact)
    activation = (preact * logistic).astype(jnp.bfloat16)
    act_grad = jnp.einsum("ng,bfg->bnf", cot, proj_weights, preferred_element_type=jnp.float32)
    pre_grad = (act_grad * logistic * (1.0 + preact * (1.0 - logistic))).astype(jnp.bfloat16)
    out_cells = jnp.einsum(
        "bnf,bfg->ng", activation, proj_weights, preferred_element_type=jnp.float32
    ).astype(jnp.bfloat16)

    chips = shares // 2
    per = chips // branches
    part, side = width // per, width // 2
    pieces = activation.reshape(branches, rows, per, part).transpose(0, 2, 1, 3)
    sent = jnp.concatenate([pre_grad.reshape(branches * rows, width), cot], axis=0)
    incoming, full_cot, slices = ring_gather(
        sent, -(-sent.shape[0] // CHUNKS // 16) * 16, 0, pieces.reshape(chips, rows, part), branches * rows
    )
    incoming = incoming.reshape(shares, branches, rows, width)
    core = lax.rem(lax.axis_index("chan"), 2)
    cot_side = lax.dynamic_slice_in_dim(full_cot, core * side, side, axis=2)
    proj_part = jnp.einsum(
        "xnf,xng->fg", slices, cot_side, preferred_element_type=jnp.float32
    )
    proj_part = jnp.concatenate([proj_part[: part // 2], proj_part[part // 2 :]], axis=1)
    group = bands * dps
    point_sum = jnp.einsum("xbnk,xbnf->bkf", spread, incoming, preferred_element_type=jnp.float32)
    spread_grad = jnp.einsum(
        "xbnf,bkf->bxnk", incoming, point_weights, preferred_element_type=jnp.float32
    ).astype(jnp.bfloat16)
    grad_in = spread_grad[0].astype(jnp.float32)
    depth_sums = []
    for level in range(1, branches):
        branch_grad = spread_grad[level].astype(jnp.float32)
        grad_padded = jnp.pad(spread_grad[level], pads)
        for i in range(3):
            for j in range(3):
                left, top = (j - 1) * level * col_step, (i - 1) * level * row_step
                tap = window(padded, 3 * col_step + left, 3 * row_step + top, cols, rows)
                depth_sums.append(jnp.sum(tap.astype(jnp.float32) * branch_grad, axis=(0, 1)))
                grad_tap = window(
                    grad_padded, 3 * col_step - left, 3 * row_step - top, cols, rows
                )
                grad_in = grad_in + grad_tap.astype(jnp.float32) * weights[level - 1, i, j]
    returned = grad_in.astype(jnp.bfloat16).transpose(1, 0, 2).reshape(bands, area, channels)
    out_cells = out_cells.reshape(bands, half, width)
    leaving = jnp.concatenate(
        [returned, out_cells[:, :, :channels], out_cells[:, :, channels:]], axis=1
    )
    taps = len(depth_sums)
    depth_part = jnp.pad(jnp.stack(depth_sums), ((0, group - taps), (0, width - channels)))
    height = branches * channels // group
    take = part // 2 // group
    terms = point_sum.astype(jnp.bfloat16).reshape(dps, bands, height, width)
    extra = jnp.concatenate(
        [proj_part.reshape(group, take, width), jnp.pad(depth_part[:, None], ((0, 0), (0, 1), (0, 0)))],
        axis=1,
    ).astype(jnp.bfloat16)
    leaving, terms, extra = lax.optimization_barrier((leaving, terms, extra))
    returned = exchange(leaving, "row")
    output = jnp.concatenate(
        [returned[:, area : area + half], returned[:, area + half :]], axis=2
    )
    output = output.reshape(ROW_CLASSES, COL_CLASSES, half, width).transpose(2, 0, 1, 3)
    output = output.reshape(1, band_rows, COL_CLASSES, width)
    grad_input = returned[:, :area].reshape(ROW_CLASSES, COL_CLASSES, half, cols, channels)
    grad_input = grad_input.transpose(2, 0, 3, 1, 4).reshape(features_in.shape)

    summed, sides, grad_proj = group_sum(
        terms, extra.reshape(dps, bands, take + 2, width), take, 1
    )
    grad_point = summed.reshape(point_weights.shape).astype(jnp.float32) * weight_scale
    grad_depth = sides.reshape(group, take + 2, width)[:taps, take, :channels]
    grad_depth = grad_depth.reshape(depth_weights.shape).astype(jnp.float32) * weight_scale
    grad_proj = grad_proj.reshape(branches, per, 2, part // 2, 2, side).transpose(0, 1, 4, 3, 2, 5)
    grad_proj = grad_proj.reshape(branches, width, width).astype(jnp.float32) * weight_scale
    return (output, grad_input, grad_depth, grad_point, grad_proj)


def solution(mesh):
    in_specs = (
        P("dp", "row", None, "chan"),
        P(None, None, None, "chan"),
        P(None, "chan", None),
        P(),
        P("dp", "row", "chan", None),
    )
    out_specs = (
        P("dp", "row", "chan", None),
        P("dp", "row", None, "chan"),
        P(None, None, None, "chan"),
        P(None, "chan", None),
        P(),
    )
    return jax.shard_map(
        on_device, mesh=mesh, in_specs=in_specs, out_specs=out_specs, check_vma=False
    )
```
